32 devices in a mesh: groups: 2 (over y), blk: 4 (over z), head: 4 (over x, core).
Axes of the slice: x: 2, y: 2, z: 4, core: 2. Of those that a mesh axis runs over, the one named last changes fastest.
Arguments:
- queries: bfloat16 [4096, 4096], P(('groups', 'blk', 'head')), parts along dimension 0, may hold values from -8 to 8
- keys: bfloat16 [4096, 4096], P(('groups', 'blk', 'head')), parts along dimension 0, may hold values from -8 to 8
- values: bfloat16 [4096, 4096], P(('groups', 'blk', 'head')), parts along dimension 0, may hold values from -6 to 6
- scale_qk: float32 [4096], replicated, may hold values from 0.7 to 8
- w_out: bfloat16 [4096, 4096], P('head'), may hold values from -0.09375 to 0.09375
- stretch_start: int32 [32], P(('groups', 'blk', 'head')), parts along dimension 0, may hold values from 0 to 1920, as said below
Outputs:
- attended: bfloat16 [4096, 4096], P(('groups', 'blk', 'head')), parts along dimension 0
The draws below stay inside these ranges and needn't reach their ends.
There are 2 independent parts, one for each index of `groups`. The reference program is written for one: setup_inputs(seed, part) draws one part's arguments, and reference() takes and returns one part's arrays. A program takes and returns all parts, laid end to end along the dimension named above; an argument that names none is the same for every part. Nothing has to cross between parts.
Inputs may be any that keep to these rules, and one draw needn't show every extreme that they name: stretch_start[b * 4 + h] = (((b + r) % 4) * 4 + h) * 128 for an offset r of 0 to 3 drawn from the seed.
All inputs are finite; a program needn't handle non-finite values.
Results may differ from the reference program's by a relative error of at most 0.04.
Values may be sent and summed in bfloat16 or wider, within the bound.
A program may use at most 128 MiB of HBM per device.

```python
import jax
import jax.numpy as jnp
from jax import lax

D = 4096
H = 32
DH = 128
TOK_DEV = 128
SEGMENTS = 4
HEAD_GROUPS = 4
SEG = 512
WIN = 1024
SEQ = 2048
HL = 8


def paired(key):
    base_q = jax.random.normal(jax.random.fold_in(key, 11), (SEQ, H * DH), jnp.float32)
    base_k = jax.random.normal(jax.random.fold_in(key, 12), (SEQ, H * DH), jnp.float32)
    return (jnp.clip(base_q, -8.0, 8.0), jnp.clip(base_k, -8.0, 8.0))


def draw_queries(key, part):
    return paired(key)[0].astype(jnp.bfloat16)


def draw_keys(key, part):
    return paired(key)[1].astype(jnp.bfloat16)


def draw_scale_qk(key, part):
    return jax.random.uniform(key, (H * DH,), jnp.float32, 0.7, 1.4)


def draw_stretch_start(key, part):
    halves = jax.random.randint(jax.random.fold_in(key, 21), (), 0, SEGMENTS // 2).astype(jnp.int32)
    offset = (halves * 2 + jnp.asarray(part, jnp.int32) % 2).astype(jnp.int32)
    order = (jnp.arange(SEGMENTS, dtype=jnp.int32) + offset) % SEGMENTS
    inner = jnp.arange(HEAD_GROUPS, dtype=jnp.int32)
    starts = (order[:, None] * HEAD_GROUPS + inner[None, :]) * TOK_DEV
    return starts.reshape(-1).astype(jnp.int32)


def steps_of(own_key, shape, cuts, low, top_value):
    def one(position, shards_of):
        draws = jax.random.uniform(jax.random.fold_in(jax.random.fold_in(own_key, 6), position), (shards_of,), jnp.float32, low / len(cuts), top_value / len(cuts))
        return jnp.repeat(jnp.exp(draws), shape[position] // shards_of).reshape((-1,) + (1,) * (len(shape) - position - 1))

    gain = one(*cuts[0])
    for cut in cuts[1:]:
        gain = gain * one(*cut)
    return gain


def bell_draw(key, dims, scale, bound, split=(), kind=jnp.bfloat16):
    loudness = steps_of(key, dims, split, -0.22, 0.18) if split else 1.0
    result = jax.random.normal(key, dims, jnp.float32) * scale * loudness
    return jnp.minimum(jnp.maximum(result, -bound), bound).astype(kind)


def setup_inputs(seed: int = 0, part: int = 0) -> dict:
    key_of = jax.random.split(jax.random.key(seed), 7)
    part_splits = jax.random.split(jax.random.fold_in(key_of[6], part), 7)
    return {
        "queries": draw_queries(jax.random.fold_in(jax.random.fold_in(key_of[6], part), 71), part),
        "keys": draw_keys(jax.random.fold_in(jax.random.fold_in(key_of[6], part), 71), part),
        "values": bell_draw(part_splits[2], (SEQ, H * DH), 1.0, 6.0, ((0, 16),)),
        "scale_qk": draw_scale_qk(jax.random.fold_in(key_of[6], 71), part),
        "w_out": bell_draw(key_of[4], (H * DH, D), (H * DH) ** -0.5, 0.09375, ((0, 4),)),
        "stretch_start": draw_stretch_start(jax.random.fold_in(jax.random.fold_in(key_of[6], part), 71), part),
    }


def normalize(rows, scale_qk):
    x = rows.astype(jnp.float32).reshape(rows.shape[0], H, DH)
    x = x * lax.rsqrt(lax.optimization_barrier(jnp.mean(x * x, axis=2, keepdims=True)) + 1e-06)
    return (x.reshape(rows.shape[0], H * DH) * scale_qk[None, :]).astype(jnp.bfloat16)

def reference(queries, keys, values, scale_qk, w_out, stretch_start):
    qn = normalize(queries, scale_qk)
    kn = normalize(keys, scale_qk)
    offsets = jnp.arange(TOK_DEV, dtype=jnp.int32)
    pos = (stretch_start[:, None] + offsets[None, :]).reshape(-1).astype(jnp.int32)
    order = jnp.argsort(pos).astype(jnp.int32)
    q_sorted = qn[order]
    k_sorted = jnp.concatenate([jnp.zeros((WIN, H * DH), jnp.bfloat16), kn[order]], axis=0)
    v_sorted = jnp.concatenate([jnp.zeros((WIN, H * DH), jnp.bfloat16), values[order]], axis=0)
    sorted_pos = pos[order]
    padded_pos = jnp.concatenate([jnp.full((WIN,), -3 * WIN, jnp.int32), sorted_pos], axis=0)
    blocks = SEQ // SEG
    inverse = 1.0 / DH ** 0.5

    def block_out(index):
        head = index // blocks
        block = index % blocks
        first_col = (head * DH).astype(jnp.int32)
        first_row = (block * SEG).astype(jnp.int32)
        q_head = lax.dynamic_slice(q_sorted, (first_row, first_col), (SEG, DH))
        k_head = lax.dynamic_slice(k_sorted, (first_row, first_col), (WIN + SEG, DH))
        v_head = lax.dynamic_slice(v_sorted, (first_row, first_col), (WIN + SEG, DH))
        q_pos = lax.dynamic_slice_in_dim(sorted_pos, first_row, SEG, 0)
        k_pos = lax.dynamic_slice_in_dim(padded_pos, first_row, WIN + SEG, 0)
        allowed = (k_pos[None, :] <= q_pos[:, None]) & (q_pos[:, None] - k_pos[None, :] < WIN)
        scores = jnp.dot(q_head, k_head.T, preferred_element_type=jnp.float32) * inverse
        peak = lax.optimization_barrier(jnp.max(jnp.where(allowed, scores, -1e+30), axis=1, keepdims=True))
        weights = jnp.where(allowed, jnp.exp(scores - peak), jnp.float32(0.0))
        total = lax.optimization_barrier(jnp.sum(weights, axis=1, keepdims=True))
        mixed = jnp.dot(weights.astype(jnp.bfloat16), v_head, preferred_element_type=jnp.float32)
        return (mixed / total).astype(jnp.bfloat16)
    stacked = lax.map(block_out, jnp.arange(H * blocks, dtype=jnp.int32))
    stacked = stacked.reshape(H, SEQ, DH)
    sorted_out = jnp.transpose(stacked, (1, 0, 2)).reshape(SEQ, H * DH)
    heads_out = sorted_out[pos]
    width = HL * DH
    summed = jnp.zeros((SEQ, D), jnp.float32)
    for group in range(HEAD_GROUPS):
        part = jnp.dot(heads_out[:, group * width:(group + 1) * width], w_out[group * width:(group + 1) * width, :], preferred_element_type=jnp.float32)
        part = lax.optimization_barrier(part.astype(jnp.bfloat16))
        summed = summed + part.astype(jnp.float32)
    return summed.astype(jnp.bfloat16)
```

```python
import functools

import jax
import jax.numpy as jnp
from jax import lax
from jax.experimental import pallas as pl
from jax.experimental.pallas import tpu as pltpu
from jax.sharding import PartitionSpec as P

DH = 128
LOG2E = 1.4426950408889634
SCORE = LOG2E / DH**0.5
NC = 2
NS = 2


def kernel(
    nh, nb, q_hbm, k_hbm, v_hbm, scale_ref, w_hbm, start_ref, rbuf,
    qin, kin, qn, kn, w_ref, qseg, kbuf, vbuf, acc, ho, sib_out, sib_in, comb,
    load_sem, loc_sem, keep_sem, a2a_s, a2a_r, h1_s, h1_r, h2_s, h2_r, sib_s, sib_r, red_s, red_r,
):
    t, hd = qin.shape
    cols = hd // nh
    heads = cols // DH
    seg = nh * t
    sub = t // NS
    width = w_ref.shape[1]
    half = width // 2
    chunk = half // NC
    nx = nh // 2
    me = lax.axis_index("head")
    z = lax.axis_index("blk")
    chip = me // 2
    core = me % 2
    sib = chip * 2 + (1 - core)
    nxt = (z + 1) % nb
    prv = (z + nb - 1) % nb

    def partner(jx, jc):
        return ((chip + jx) % nx) * 2 + (core + jc) % 2

    others = [(jx, 0) for jx in range(1, nx)] + [(jx, 1) for jx in range(nx)]
    arrival = [(jx, jc) for jx in range(nx) for jc in range(2) if jx or jc]

    loads = [
        pltpu.make_async_copy(k_hbm, kin, load_sem.at[0]),
        pltpu.make_async_copy(q_hbm, qin, load_sem.at[1]),
        pltpu.make_async_copy(w_hbm, w_ref, load_sem.at[2]),
    ]
    for copy in loads:
        copy.start()

    barrier = pltpu.get_barrier_semaphore()
    for jx, jc in others:
        pl.semaphore_signal(barrier, inc=1, device_id={"head": partner(jx, jc)})
    pl.semaphore_signal(barrier, inc=1, device_id={"blk": nxt})
    pl.semaphore_signal(barrier, inc=1, device_id={"blk": prv})
    pl.semaphore_wait(barrier, nh + 1)

    def group(ref, peer):
        return ref.at[:, pl.ds(pl.multiple_of(peer * cols, DH), cols)]

    def piece(ref, base, index):
        return ref.at[pl.ds(pl.multiple_of(base + index * t, t), t), :]

    def swap(kind, src, dst, base, peer, source):
        return pltpu.make_async_remote_copy(
            src_ref=group(src, peer), dst_ref=piece(dst, base, source),
            send_sem=a2a_s.at[kind, peer], recv_sem=a2a_r.at[kind, source],
            device_id={"head": peer},
        )

    def hop(src, dst, kind, base, index, send, recv):
        return pltpu.make_async_remote_copy(
            src_ref=src, dst_ref=piece(dst, base, index),
            send_sem=send.at[kind, index], recv_sem=recv.at[kind, index],
            device_id={"blk": nxt},
        )

    def normed(src, dst, peer):
        for h in range(heads):
            at = pl.ds(pl.multiple_of(peer * cols + h * DH, DH), DH)
            x = src[:, at].astype(jnp.float32)
            x = x * lax.rsqrt(jnp.mean(x * x, axis=1, keepdims=True) + 1e-06)
            dst[:, at] = (x * scale_ref[:, at]).astype(jnp.bfloat16)

    hop(group(v_hbm, me), vbuf, 1, seg, me, h1_s, h1_r).start()
    for jx, jc in others:
        swap(1, v_hbm, vbuf, 2 * seg, partner(jx, jc), me).start()
    own_v = pltpu.make_async_copy(group(v_hbm, me), piece(vbuf, 2 * seg, me), loc_sem.at[1])
    own_v.start()

    loads[0].wait()
    normed(kin, kn, me)
    hop(group(kn, me), kbuf, 0, seg, me, h1_s, h1_r).start()
    own_k = pltpu.make_async_copy(group(kn, me), piece(kbuf, 2 * seg, me), loc_sem.at[0])
    own_k.start()
    for jx, jc in others:
        peer = partner(jx, jc)
        normed(kin, kn, peer)
        swap(0, kn, kbuf, 2 * seg, peer, me).start()

    loads[1].wait()
    for jx, jc in [(0, 0)] + others:
        normed(qin, qn, partner(jx, jc))
    own_q = pltpu.make_async_copy(group(qn, me), piece(qseg, 0, me), loc_sem.at[2])
    own_q.start()

    def onward(kind, src, buf, jx, jc):
        source = partner(jx, jc)
        swap(kind, src, buf, 2 * seg, source, source).wait_recv()
        hop(piece(buf, 2 * seg, source), buf, kind, seg, source, h1_s, h1_r).start()

    onward(1, v_hbm, vbuf, 0, 1)
    onward(0, kn, kbuf, 0, 1)
    for jx, jc in arrival[1:]:
        onward(1, v_hbm, vbuf, jx, jc)
    for jx, jc in arrival[1:]:
        onward(0, kn, kbuf, jx, jc)
    for jx, jc in others:
        peer = partner(jx, jc)
        swap(2, qn, qseg, 0, peer, me).start()

    def slab(ref, base, i, part):
        return ref.at[pl.ds(pl.multiple_of(base + i * t + part * sub, sub), sub), :]

    def pass_on(kind, buf, i, part):
        return pltpu.make_async_remote_copy(
            src_ref=slab(buf, seg, i, part), dst_ref=slab(buf, 0, i, part),
            send_sem=h2_s.at[kind, i, part], recv_sem=h2_r.at[kind, i, part],
            device_id={"blk": nxt},
        )

    def relay(step, carry):
        i = nh - 1 - step
        for kind, buf in ((0, kbuf), (1, vbuf)):
            hop(piece(buf, 2 * seg, i), buf, kind, seg, i, h1_s, h1_r).wait_recv()
        for part in reversed(range(NS)):
            for kind, buf in ((0, kbuf), (1, vbuf)):
                pass_on(kind, buf, i, part).start()
        return carry

    lax.fori_loop(0, nh, relay, 0)
    for jx, jc in arrival:
        source = partner(jx, jc)
        swap(2, qn, qseg, 0, source, source).wait_recv()
    own_q.wait()
    own_k.wait()
    own_v.wait()
    loads[2].wait()

    first = start_ref[0] - me * t
    row = lax.broadcasted_iota(jnp.int32, (t, 2 * seg), 0)
    col = lax.broadcasted_iota(jnp.int32, (t, 2 * seg), 1)

    def to_sibling(i, part, c):
        at = (i, pl.ds(part * sub, sub), pl.ds(c * chunk, chunk))
        return pltpu.make_async_remote_copy(
            src_ref=sib_out.at[at], dst_ref=sib_in.at[at],
            send_sem=sib_s.at[i, part, c], recv_sem=sib_r.at[i, part, c],
            device_id={"head": sib},
        )

    def home(x, side, part, c):
        columns = pl.ds(pl.multiple_of(side * half + c * chunk, DH), chunk)
        return rbuf.at[x, pl.ds(part * sub, sub), columns]

    def to_owner(i, part, c, source, owner):
        return pltpu.make_async_remote_copy(
            src_ref=comb.at[i, pl.ds(part * sub, sub), pl.ds(c * chunk, chunk)],
            dst_ref=home(source // 2, source % 2, part, c),
            send_sem=red_s.at[i, part, c], recv_sem=red_r.at[source, part, c],
            device_id={"head": owner},
        )

    def keep(i, part, c):
        return pltpu.make_async_copy(
            comb.at[i, pl.ds(part * sub, sub), pl.ds(c * chunk, chunk)],
            home(chip, core, part, c), keep_sem.at[part, c],
        )

    def block(step, carry):
        i = nh - 1 - step
        rows = pl.ds(pl.multiple_of(i * t, t), t)
        keys = pl.ds(pl.multiple_of(i * t + t, t), 2 * seg)
        oldest = 2 * seg - first - i * t
        allowed = (col <= row + (2 * seg - t)) & (col >= oldest - t)
        held = []
        for h in range(heads):
            at = pl.ds(h * DH, DH)
            s = lax.dot_general(
                qseg[rows, at], kbuf[keys, at], (((1,), (1,)), ((), ())),
                preferred_element_type=jnp.float32,
            )
            s = jnp.where(allowed, s, -1e30)
            peak = jnp.max(s, axis=1, keepdims=True)
            p = jnp.exp2((s - peak) * SCORE)
            held.append((peak, jnp.sum(p, axis=1, keepdims=True)))
            acc[:, at] = jnp.dot(
                p.astype(jnp.bfloat16), vbuf[keys, at], preferred_element_type=jnp.float32
            )

        for part in reversed(range(NS)):
            for kind, buf in ((0, kbuf), (1, vbuf)):
                pass_on(kind, buf, i, part).wait_recv()
            low = part * sub
            many = t - low
            keys = pl.ds(pl.multiple_of(i * t + low, sub), many)
            here = pl.ds(pl.multiple_of(i * t + low, sub), sub)
            age = lax.broadcasted_iota(jnp.int32, (sub, many), 1)
            allowed = (age > lax.broadcasted_iota(jnp.int32, (sub, many), 0)) & (
                age >= oldest - low
            )
            for h in range(heads):
                at = pl.ds(h * DH, DH)
                s = lax.dot_general(
                    qseg[here, at], kbuf[keys, at], (((1,), (1,)), ((), ())),
                    preferred_element_type=jnp.float32,
                )
                s = jnp.where(allowed, s, -1e30)
                peak, total = (value[low:low + sub] for value in held[h])
                top = jnp.maximum(peak, jnp.max(s, axis=1, keepdims=True))
                p = jnp.exp2((s - top) * SCORE)
                fade = jnp.exp2((peak - top) * SCORE)
                total = total * fade + jnp.sum(p, axis=1, keepdims=True)
                o = acc[pl.ds(low, sub), at] * fade + jnp.dot(
                    p.astype(jnp.bfloat16), vbuf[keys, at], preferred_element_type=jnp.float32
                )
                ho[pl.ds(low, sub), at] = (o / total).astype(jnp.bfloat16)

            spot = pl.ds(low, sub)

            def project(side, c):
                at = pl.ds(pl.multiple_of(side * half + c * chunk, DH), chunk)
                return jnp.dot(ho[spot, :], w_ref[:, at], preferred_element_type=jnp.float32)

            for c in range(NC):
                sib_out[i, spot, pl.ds(c * chunk, chunk)] = project(1 - core, c).astype(
                    jnp.bfloat16
                )
                to_sibling(i, part, c).start()
            for c in range(NC):
                at = pl.ds(c * chunk, chunk)
                mine = project(core, c)
                to_sibling(i, part, c).wait_recv()
                both = mine + sib_in[i, spot, at].astype(jnp.float32)
                comb[i, spot, at] = both.astype(jnp.bfloat16)

                @pl.when(me == i)
                def _():
                    keep(i, part, c).start()

                @pl.when(me != i)
                def _():
                    to_owner(i, part, c, me, i).start()

        return carry

    lax.fori_loop(0, nh, block, 0)

    pieces = [(part, c) for part in reversed(range(NS)) for c in range(NC)]
    for part, c in pieces:
        keep(me, part, c).wait()
        for jx, jc in arrival:
            source = partner(jx, jc)
            to_owner(source, part, c, source, source).wait_recv()

    for jx, jc in arrival:
        peer = partner(jx, jc)
        swap(1, v_hbm, vbuf, 2 * seg, peer, me).wait_send()
        swap(0, kn, kbuf, 2 * seg, peer, me).wait_send()
        swap(2, qn, qseg, 0, peer, me).wait_send()
        for part, c in pieces:
            to_owner(peer, part, c, me, peer).wait_send()

    def sent(i, carry):
        for kind, buf in ((0, kbuf), (1, vbuf)):
            hop(piece(buf, 2 * seg, i), buf, kind, seg, i, h1_s, h1_r).wait_send()
            for part in range(NS):
                pass_on(kind, buf, i, part).wait_send()
        for part, c in pieces:
            to_sibling(i, part, c).wait_send()
        return carry

    lax.fori_loop(0, nh, sent, 0)


def line_kernel(
    sides, q_hbm, k_hbm, v_hbm, scale_ref, w_hbm, start_ref, rbuf,
    qin, kin, qn, kn, w_ref, qseg, kbuf, vbuf, gq, go, gin, gst, gst_in, turn,
    acc, ho, sib_out, sib_in, comb,
    load_sem, loc_sem, keep_sem, a2a_s, a2a_r, kv_s, kv_r, rl_s, gq_s, gq_r,
    go_s, go_r, st_s, st_r, own_s, sib_s, sib_r, red_s, red_r,
):
    nh, nb = 4, 4
    t, hd = qin.shape
    cols = hd // nh
    heads = cols // DH
    seg = nh * t
    width = w_ref.shape[1]
    half = width // 2
    chunk = half // NC
    nx = nh // 2
    me = lax.axis_index("head")
    z = lax.axis_index("blk")
    y = lax.axis_index("groups")
    late = sides[0] + y * (sides[1] - sides[0])
    chip = me // 2
    core = me % 2
    sib = chip * 2 + (1 - core)

    asks = (z == 3) | ((z == 2) & (late == 0)) | ((z == 0) & (late == 1))
    ask_slot = jnp.where(z == 3, 0, 1)
    ask_to = jnp.where(z == 2, 1, 2)
    jobs = jnp.where(z == 1, 2 - late, jnp.where(z == 2, 1 + late, 0))
    helped = asks | (z == 1)

    def partner(jx, jc):
        return ((chip + jx) % nx) * 2 + (core + jc) % 2

    others = [(jx, 0) for jx in range(1, nx)] + [(jx, 1) for jx in range(nx)]
    arrival = [(jx, jc) for jx in range(nx) for jc in range(2) if jx or jc]

    loads = [
        pltpu.make_async_copy(k_hbm, kin, load_sem.at[0]),
        pltpu.make_async_copy(q_hbm, qin, load_sem.at[1]),
        pltpu.make_async_copy(w_hbm, w_ref, load_sem.at[2]),
    ]
    for copy in loads:
        copy.start()

    barrier = pltpu.get_barrier_semaphore()
    for jx, jc in others:
        pl.semaphore_signal(barrier, inc=1, device_id={"head": partner(jx, jc)})
    for d in range(1, nb):
        pl.semaphore_signal(barrier, inc=1, device_id={"blk": (z + d) % nb})
    pl.semaphore_wait(barrier, nh + nb - 2)

    def group(ref, peer):
        return ref.at[:, pl.ds(pl.multiple_of(peer * cols, DH), cols)]

    def piece(ref, base, index):
        return ref.at[pl.ds(pl.multiple_of(base + index * t, t), t), :]

    def swap(kind, src, dst, base, peer, source):
        return pltpu.make_async_remote_copy(
            src_ref=group(src, peer), dst_ref=piece(dst, base, source),
            send_sem=a2a_s.at[kind, peer], recv_sem=a2a_r.at[kind, source],
            device_id={"head": peer},
        )

    far = jnp.where(z == 3, 1, 0)
    hop_base = jnp.where(z == 3, 0, seg)
    hop_to = jnp.where(z == 3, 1, z + 1)

    def hop(src, dst, kind, index):
        return pltpu.make_async_remote_copy(
            src_ref=src, dst_ref=piece(dst, hop_base, index),
            send_sem=kv_s.at[kind, index], recv_sem=kv_r.at[far, kind, index],
            device_id={"blk": hop_to},
        )

    def landed(dst, slot, kind, index):
        return pltpu.make_async_remote_copy(
            src_ref=piece(dst, (1 - slot) * seg, index), dst_ref=piece(dst, (1 - slot) * seg, index),
            send_sem=kv_s.at[kind, index], recv_sem=kv_r.at[slot, kind, index],
            device_id={"blk": hop_to},
        )

    def relay(dst, kind, index):
        return pltpu.make_async_remote_copy(
            src_ref=piece(dst, 0, index), dst_ref=piece(dst, seg, index),
            send_sem=rl_s.at[kind, index], recv_sem=kv_r.at[0, kind, index],
            device_id={"blk": 0},
        )

    def normed(src, dst, peer):
        for h in range(heads):
            at = pl.ds(pl.multiple_of(peer * cols + h * DH, DH), DH)
            x = src[:, at].astype(jnp.float32)
            x = x * lax.rsqrt(jnp.mean(x * x, axis=1, keepdims=True) + 1e-06)
            dst[:, at] = (x * scale_ref[:, at]).astype(jnp.bfloat16)

    bufs = (kbuf, vbuf)

    def pass_back(kind, index):
        @pl.when(z == 1)
        def _():
            landed(bufs[kind], 1, kind, index).wait_recv()
            relay(bufs[kind], kind, index).start()

    hop(group(v_hbm, me), vbuf, 1, me).start()
    for jx, jc in others:
        swap(1, v_hbm, vbuf, 2 * seg, partner(jx, jc), me).start()
    own_v = pltpu.make_async_copy(group(v_hbm, me), piece(vbuf, 2 * seg, me), loc_sem.at[1])
    own_v.start()

    loads[0].wait()
    normed(kin, kn, me)
    hop(group(kn, me), kbuf, 0, me).start()
    own_k = pltpu.make_async_copy(group(kn, me), piece(kbuf, 2 * seg, me), loc_sem.at[0])
    own_k.start()
    for jx, jc in others:
        peer = partner(jx, jc)
        normed(kin, kn, peer)
        swap(0, kn, kbuf, 2 * seg, peer, me).start()

    loads[1].wait()
    for jx, jc in [(0, 0)] + others:
        normed(qin, qn, partner(jx, jc))
    own_q = pltpu.make_async_copy(group(qn, me), piece(qseg, 0, me), loc_sem.at[2])
    own_q.start()

    def onward(kind, src, buf, jx, jc):
        source = partner(jx, jc)
        swap(kind, src, buf, 2 * seg, source, source).wait_recv()
        hop(piece(buf, 2 * seg, source), buf, kind, source).start()

    onward(1, v_hbm, vbuf, 0, 1)
    onward(0, kn, kbuf, 0, 1)
    pass_back(1, me)
    pass_back(0, me)
    for jx, jc in arrival[1:]:
        onward(1, v_hbm, vbuf, jx, jc)
    pass_back(1, sib)
    pass_back(0, sib)
    for jx, jc in arrival[1:]:
        onward(0, kn, kbuf, jx, jc)
    for jx, jc in others:
        peer = partner(jx, jc)
        swap(2, qn, qseg, 0, peer, me).start()
    for kind in (1, 0):
        for jx, jc in arrival[1:]:
            pass_back(kind, partner(jx, jc))

    for jx, jc in arrival:
        source = partner(jx, jc)
        swap(2, qn, qseg, 0, source, source).wait_recv()
    own_q.wait()
    own_k.wait()
    own_v.wait()
    loads[2].wait()

    def turn_of(step):
        return (step % 2) * 2 + step // 2

    def ask(i):
        return pltpu.make_async_remote_copy(
            src_ref=piece(qseg, 0, i), dst_ref=piece(gq.at[ask_slot], 0, i),
            send_sem=gq_s.at[i], recv_sem=gq_r.at[ask_slot, i],
            device_id={"blk": ask_to},
        )

    mine_q = pltpu.make_async_copy(qseg, gq.at[0], own_s.at[0])

    @pl.when(z == 1)
    def _():
        mine_q.start()

    def hop_sent(i, carry):
        for kind in range(2):
            hop(piece(bufs[kind], 2 * seg, i), bufs[kind], kind, i).wait_send()
        return carry

    lax.fori_loop(0, nh, hop_sent, 0)

    @pl.when(asks)
    def _():
        def send(step, carry):
            ask(turn_of(step)).start()
            return carry

        lax.fori_loop(0, nh, send, 0)

    def prev_in(i, carry):
        for kind in range(2):
            landed(bufs[kind], 0, kind, i).wait_recv()
        return carry

    lax.fori_loop(0, nh, prev_in, 0)

    @pl.when(z == 1)
    def _():
        mine_q.wait()

    @pl.when(jnp.logical_not(helped))
    def _():
        gin[...] = jnp.zeros_like(gin)
        gst_in[...] = jnp.full_like(gst_in, -1e30)

    turn[...] = jnp.zeros_like(turn)

    first = start_ref[0] - me * t
    row = lax.broadcasted_iota(jnp.int32, (t, 2 * seg), 0)
    col = lax.broadcasted_iota(jnp.int32, (t, 2 * seg), 1)
    short_row = lax.broadcasted_iota(jnp.int32, (t, seg), 0)
    short_col = lax.broadcasted_iota(jnp.int32, (t, seg), 1)
    lane = lax.broadcasted_iota(jnp.int32, (t, DH), 1)

    def answer(e, i):
        to = jnp.where(e == 0, 3, jnp.where(z == 1, 2, 0))
        return [
            pltpu.make_async_remote_copy(
                src_ref=piece(go.at[e], 0, i), dst_ref=piece(gin, 0, i),
                send_sem=go_s.at[e, i], recv_sem=go_r.at[i], device_id={"blk": to},
            ),
            pltpu.make_async_remote_copy(
                src_ref=gst.at[e, i], dst_ref=gst_in.at[i],
                send_sem=st_s.at[e, i], recv_sem=st_r.at[i], device_id={"blk": to},
            ),
        ]

    def own_answer(i):
        return [
            pltpu.make_async_copy(piece(go.at[0], 0, i), piece(gin, 0, i), own_s.at[1]),
            pltpu.make_async_copy(gst.at[0, i], gst_in.at[i], own_s.at[2]),
        ]

    def to_sibling(i, c):
        at = (i, slice(None), pl.ds(c * chunk, chunk))
        return pltpu.make_async_remote_copy(
            src_ref=sib_out.at[at], dst_ref=sib_in.at[at],
            send_sem=sib_s.at[i, c], recv_sem=sib_r.at[i, c],
            device_id={"head": sib},
        )

    def home(x, side, c):
        columns = pl.ds(pl.multiple_of(side * half + c * chunk, DH), chunk)
        return rbuf.at[x, :, columns]

    def to_owner(i, c, source, owner):
        return pltpu.make_async_remote_copy(
            src_ref=comb.at[i, :, pl.ds(c * chunk, chunk)],
            dst_ref=home(source // 2, source % 2, c),
            send_sem=red_s.at[i, c], recv_sem=red_r.at[source, c],
            device_id={"head": owner},
        )

    def keep(i, c):
        return pltpu.make_async_copy(
            comb.at[i, :, pl.ds(c * chunk, chunk)], home(chip, core, c), keep_sem.at[c],
        )

    def block(step, carry):
        i = turn_of(step)
        rows = pl.ds(pl.multiple_of(i * t, t), t)

        def help_with(e, inner):
            remote = (z != 1) | (e != 0)

            @pl.when(remote)
            def _():
                pltpu.make_async_remote_copy(
                    src_ref=piece(gq.at[e], 0, i), dst_ref=piece(gq.at[e], 0, i),
                    send_sem=gq_s.at[i], recv_sem=gq_r.at[e, i], device_id={"blk": ask_to},
                ).wait_recv()

            base = jnp.where(z == 1, e * seg, (e + 1) * seg)
            keys = pl.ds(pl.multiple_of(base, seg), seg)
            allowed = short_col > short_row + i * t
            logs = jnp.zeros((t, DH), jnp.float32)
            for h in range(heads):
                at = pl.ds(h * DH, DH)
                s = lax.dot_general(
                    gq[e, rows, at], kbuf[keys, at], (((1,), (1,)), ((), ())),
                    preferred_element_type=jnp.float32,
                )
                s = jnp.where(allowed, s, -1e30)
                peak = jnp.max(s, axis=1, keepdims=True)
                p = jnp.exp2((s - peak) * SCORE)
                total = jnp.sum(p, axis=1, keepdims=True)
                o = jnp.dot(
                    p.astype(jnp.bfloat16), vbuf[keys, at], preferred_element_type=jnp.float32
                )
                go[e, rows, at] = (o / total).astype(jnp.bfloat16)
                logs = jnp.where(lane == h, peak * SCORE + jnp.log(total) * LOG2E, logs)
            gst[e, i] = logs.T[:heads]

            @pl.when(remote)
            def _():
                for copy in answer(e, i):
                    copy.start()

            @pl.when(jnp.logical_not(remote))
            def _():
                for copy in own_answer(i):
                    copy.start()

            return inner

        lax.fori_loop(0, jobs, help_with, 0)

        keys = pl.ds(seg, 2 * seg)
        allowed = (col <= row + (seg + i * t)) & (col >= seg - first)
        held = []
        for h in range(heads):
            at = pl.ds(h * DH, DH)
            s = lax.dot_general(
                qseg[rows, at], kbuf[keys, at], (((1,), (1,)), ((), ())),
                preferred_element_type=jnp.float32,
            )
            s = jnp.where(allowed, s, -1e30)
            peak = jnp.max(s, axis=1, keepdims=True)
            p = jnp.exp2((s - peak) * SCORE)
            held.append((peak * SCORE, jnp.sum(p, axis=1, keepdims=True)))
            acc[:, at] = jnp.dot(
                p.astype(jnp.bfloat16), vbuf[keys, at], preferred_element_type=jnp.float32
            )

        @pl.when(z == 1)
        def _():
            for copy in own_answer(i):
                copy.wait()

        @pl.when(asks)
        def _():
            for copy in answer(0, i):
                copy.wait_recv()

        turn[:heads] = jnp.where(first >= 2 * seg, gst_in[i], -1e30)
        logs = turn[...].T
        for h in range(heads):
            at = pl.ds(h * DH, DH)
            peak, total = held[h]
            log = logs[:, h:h + 1]
            top = jnp.maximum(peak, log)
            fade = jnp.exp2(peak - top)
            gain = jnp.exp2(log - top)
            o = acc[:, at] * fade + gin[rows, at].astype(jnp.float32) * gain
            ho[:, at] = (o / (total * fade + gain)).astype(jnp.bfloat16)

        def project(side, c):
            at = pl.ds(pl.multiple_of(side * half + c * chunk, DH), chunk)
            return jnp.dot(ho[...], w_ref[:, at], preferred_element_type=jnp.float32)

        for c in range(NC):
            sib_out[i, :, pl.ds(c * chunk, chunk)] = project(1 - core, c).astype(jnp.bfloat16)
            to_sibling(i, c).start()
        for c in range(NC):
            at = pl.ds(c * chunk, chunk)
            mine = project(core, c)
            to_sibling(i, c).wait_recv()
            both = mine + sib_in[i, :, at].astype(jnp.float32)
            comb[i, :, at] = both.astype(jnp.bfloat16)

            @pl.when(me == i)
            def _():
                keep(i, c).start()

            @pl.when(me != i)
            def _():
                to_owner(i, c, me, i).start()

        return carry

    lax.fori_loop(0, nh, block, 0)

    for c in range(NC):
        keep(me, c).wait()
        for jx, jc in arrival:
            source = partner(jx, jc)
            to_owner(source, c, source, source).wait_recv()

    for jx, jc in arrival:
        peer = partner(jx, jc)
        swap(1, v_hbm, vbuf, 2 * seg, peer, me).wait_send()
        swap(0, kn, kbuf, 2 * seg, peer, me).wait_send()
        swap(2, qn, qseg, 0, peer, me).wait_send()
        for c in range(NC):
            to_owner(peer, c, me, peer).wait_send()

    def sent(i, carry):
        for c in range(NC):
            to_sibling(i, c).wait_send()

        @pl.when(z == 1)
        def _():
            for kind in range(2):
                relay(bufs[kind], kind, i).wait_send()

        @pl.when(asks)
        def _():
            ask(i).wait_send()

        def answered(e, inner):
            @pl.when((z != 1) | (e != 0))
            def _():
                for copy in answer(e, i):
                    copy.wait_send()

            return inner

        lax.fori_loop(0, jobs, answered, 0)
        return carry

    lax.fori_loop(0, nh, sent, 0)


def line_call(sides, queries, keys, values, scale, w_out, stretch_start):
    nh = 4
    t, hd = queries.shape
    cols = hd // nh
    seg = nh * t
    width = w_out.shape[1]
    half = width // 2
    heads = cols // DH
    bf16 = jnp.bfloat16
    f32 = jnp.float32
    dma = pltpu.SemaphoreType.DMA
    anywhere = pl.BlockSpec(memory_space=pltpu.HBM)
    vmem = pl.BlockSpec(memory_space=pltpu.VMEM)
    return pl.pallas_call(
        functools.partial(line_kernel, sides),
        out_shape=pltpu.VMEM((nh // 2, t, width), bf16),
        in_specs=[anywhere, anywhere, anywhere, vmem, anywhere,
                  pl.BlockSpec(memory_space=pltpu.SMEM)],
        out_specs=vmem,
        scratch_shapes=[
            pltpu.VMEM((t, hd), bf16),
            pltpu.VMEM((t, hd), bf16),
            pltpu.VMEM((t, hd), bf16),
            pltpu.VMEM((t, hd), bf16),
            pltpu.VMEM((cols, width), bf16),
            pltpu.VMEM((seg, cols), bf16),
            pltpu.VMEM((3 * seg, cols), bf16),
            pltpu.VMEM((3 * seg, cols), bf16),
            pltpu.VMEM((2, seg, cols), bf16),
            pltpu.VMEM((2, seg, cols), bf16),
            pltpu.VMEM((seg, cols), bf16),
            pltpu.VMEM((2, nh, heads, t), f32),
            pltpu.VMEM((nh, heads, t), f32),
            pltpu.VMEM((DH, t), f32),
            pltpu.VMEM((t, cols), f32),
            pltpu.VMEM((t, cols), bf16),
            pltpu.VMEM((nh, t, half), bf16),
            pltpu.VMEM((nh, t, half), bf16),
            pltpu.VMEM((nh, t, half), bf16),
            dma((3,)),
            dma((3,)),
            dma((NC,)),
            dma((3, nh)),
            dma((3, nh)),
            dma((2, nh)),
            dma((2, 2, nh)),
            dma((2, nh)),
            dma((nh,)),
            dma((2, nh)),
            dma((2, nh)),
            dma((nh,)),
            dma((2, nh)),
            dma((nh,)),
            dma((3,)),
            dma((nh, NC)),
            dma((nh, NC)),
            dma((nh, NC)),
            dma((nh, NC)),
        ],
        compiler_params=pltpu.CompilerParams(
            collective_id=sides[0] * 2 + sides[1], has_side_effects=True,
            vmem_limit_bytes=54 * 1024 * 1024,
        ),
    )(queries, keys, values, scale, w_out, stretch_start)


def line_parts(nb, nh, queries, keys, values, scale_qk, w_out, stretch_start):
    t, hd = queries.shape
    z = lax.axis_index("blk")
    y = lax.axis_index("groups")
    other = lax.ppermute(stretch_start, "groups", [(0, 1), (1, 0)])

    def side(start):
        offset = (start[0] // (nh * t) - z + nb) % nb
        return (offset >= 2).astype(jnp.int32)

    mine, theirs = side(stretch_start), side(other)
    which = jnp.where(y == 0, mine * 2 + theirs, theirs * 2 + mine)
    branches = [functools.partial(line_call, (a, b)) for a in range(2) for b in range(2)]
    return lax.switch(
        which, branches, queries, keys, values, scale_qk.reshape(1, hd), w_out, stretch_start
    )


def solution(mesh):
    nh = mesh.shape["head"]
    nb = mesh.shape["blk"]

    def shards(queries, keys, values, scale_qk, w_out, stretch_start):
        if nb == 4 and nh == 4 and mesh.shape["groups"] == 2:
            parts = line_parts(nb, nh, queries, keys, values, scale_qk, w_out, stretch_start)
            return jnp.sum(parts.astype(jnp.float32), axis=0).astype(jnp.bfloat16)
        t, hd = queries.shape
        cols = hd // nh
        seg = nh * t
        width = w_out.shape[1]
        half = width // 2
        bf16 = jnp.bfloat16
        dma = pltpu.SemaphoreType.DMA
        anywhere = pl.BlockSpec(memory_space=pltpu.HBM)
        vmem = pl.BlockSpec(memory_space=pltpu.VMEM)
        parts = pl.pallas_call(
            functools.partial(kernel, nh, nb),
            out_shape=pltpu.VMEM((nh // 2, t, width), bf16),
            in_specs=[anywhere, anywhere, anywhere, vmem, anywhere,
                      pl.BlockSpec(memory_space=pltpu.SMEM)],
            out_specs=vmem,
            scratch_shapes=[
                pltpu.VMEM((t, hd), bf16),
                pltpu.VMEM((t, hd), bf16),
                pltpu.VMEM((t, hd), bf16),
                pltpu.VMEM((t, hd), bf16),
                pltpu.VMEM((cols, width), bf16),
                pltpu.VMEM((seg, cols), bf16),
                pltpu.VMEM((3 * seg, cols), bf16),
                pltpu.VMEM((3 * seg, cols), bf16),
                pltpu.VMEM((t, cols), jnp.float32),
                pltpu.VMEM((t, cols), bf16),
                pltpu.VMEM((nh, t, half), bf16),
                pltpu.VMEM((nh, t, half), bf16),
                pltpu.VMEM((nh, t, half), bf16),
                dma((3,)),
                dma((3,)),
                dma((NS, NC)),
                dma((3, nh)),
                dma((3, nh)),
                dma((2, nh)),
                dma((2, nh)),
                dma((2, nh, NS)),
                dma((2, nh, NS)),
                dma((nh, NS, NC)),
                dma((nh, NS, NC)),
                dma((nh, NS, NC)),
                dma((nh, NS, NC)),
            ],
            compiler_params=pltpu.CompilerParams(
                collective_id=0, has_side_effects=True, vmem_limit_bytes=54 * 1024 * 1024
            ),
        )(queries, keys, values, scale_qk.reshape(1, hd), w_out, stretch_start)
        return jnp.sum(parts.astype(jnp.float32), axis=0).astype(bf16)

    return jax.shard_map(
        shards,
        mesh=mesh,
        in_specs=(
            P(("groups", "blk", "head"), None),
            P(("groups", "blk", "head"), None),
            P(("groups", "blk", "head"), None),
            P(),
            P("head", None),
            P(("groups", "blk", "head")),
        ),
        out_specs=P(("groups", "blk", "head"), None),
        check_vma=False,
    )
```

```python
import functools

import jax
import jax.numpy as jnp
from jax import lax
from jax.experimental import pallas as pl
from jax.experimental.pallas import tpu as pltpu
from jax.sharding import PartitionSpec as P

DH = 128
LOG2E = 1.4426950408889634
SCORE = LOG2E / DH**0.5
NC = 2
NS = 2


def kernel(
    nh, nb, q_hbm, k_hbm, v_hbm, scale_ref, w_hbm, start_ref, rbuf,
    qin, kin, qn, kn, w_ref, qseg, kbuf, vbuf, acc, ho, sib_out, sib_in, comb,
    load_sem, loc_sem, keep_sem, a2a_s, a2a_r, h1_s, h1_r, h2_s, h2_r, sib_s, sib_r, red_s, red_r,
):
    t, hd = qin.shape
    cols = hd // nh
    heads = cols // DH
    seg = nh * t
    sub = t // NS
    width = w_ref.shape[1]
    half = width // 2
    chunk = half // NC
    nx = nh // 2
    me = lax.axis_index("head")
    z = lax.axis_index("blk")
    chip = me // 2
    core = me % 2
    sib = chip * 2 + (1 - core)
    nxt = (z + 1) % nb
    prv = (z + nb - 1) % nb

    def partner(jx, jc):
        return ((chip + jx) % nx) * 2 + (core + jc) % 2

    others = [(jx, 0) for jx in range(1, nx)] + [(jx, 1) for jx in range(nx)]
    arrival = [(jx, jc) for jx in range(nx) for jc in range(2) if jx or jc]

    loads = [
        pltpu.make_async_copy(k_hbm, kin, load_sem.at[0]),
        pltpu.make_async_copy(q_hbm, qin, load_sem.at[1]),
        pltpu.make_async_copy(w_hbm, w_ref, load_sem.at[2]),
    ]
    for copy in loads:
        copy.start()

    barrier = pltpu.get_barrier_semaphore()
    for jx, jc in others:
        pl.semaphore_signal(barrier, inc=1, device_id={"head": partner(jx, jc)})
    pl.semaphore_signal(barrier, inc=1, device_id={"blk": nxt})
    pl.semaphore_signal(barrier, inc=1, device_id={"blk": prv})
    pl.semaphore_wait(barrier, nh + 1)

    def group(ref, peer):
        return ref.at[:, pl.ds(pl.multiple_of(peer * cols, DH), cols)]

    def piece(ref, base, index):
        return ref.at[pl.ds(pl.multiple_of(base + index * t, t), t), :]

    def swap(kind, src, dst, base, peer, source):
        return pltpu.make_async_remote_copy(
            src_ref=group(src, peer), dst_ref=piece(dst, base, source),
            send_sem=a2a_s.at[kind, peer], recv_sem=a2a_r.at[kind, source],
            device_id={"head": peer},
        )

    def hop(src, dst, kind, base, index, send, recv):
        return pltpu.make_async_remote_copy(
            src_ref=src, dst_ref=piece(dst, base, index),
            send_sem=send.at[kind, index], recv_sem=recv.at[kind, index],
            device_id={"blk": nxt},
        )

    def normed(src, dst, peer):
        for h in range(heads):
            at = pl.ds(pl.multiple_of(peer * cols + h * DH, DH), DH)
            x = src[:, at].astype(jnp.float32)
            x = x * lax.rsqrt(jnp.mean(x * x, axis=1, keepdims=True) + 1e-06)
            dst[:, at] = (x * scale_ref[:, at]).astype(jnp.bfloat16)

    hop(group(v_hbm, me), vbuf, 1, seg, me, h1_s, h1_r).start()
    for jx, jc in others:
        swap(1, v_hbm, vbuf, 2 * seg, partner(jx, jc), me).start()
    own_v = pltpu.make_async_copy(group(v_hbm, me), piece(vbuf, 2 * seg, me), loc_sem.at[1])
    own_v.start()

    loads[0].wait()
    normed(kin, kn, me)
    hop(group(kn, me), kbuf, 0, seg, me, h1_s, h1_r).start()
    own_k = pltpu.make_async_copy(group(kn, me), piece(kbuf, 2 * seg, me), loc_sem.at[0])
    own_k.start()
    for jx, jc in others:
        peer = partner(jx, jc)
        normed(kin, kn, peer)
        swap(0, kn, kbuf, 2 * seg, peer, me).start()

    loads[1].wait()
    for jx, jc in [(0, 0)] + others:
        normed(qin, qn, partner(jx, jc))
    own_q = pltpu.make_async_copy(group(qn, me), piece(qseg, 0, me), loc_sem.at[2])
    own_q.start()

    def onward(kind, src, buf, jx, jc):
        source = partner(jx, jc)
        swap(kind, src, buf, 2 * seg, source, source).wait_recv()
        hop(piece(buf, 2 * seg, source), buf, kind, seg, source, h1_s, h1_r).start()

    onward(1, v_hbm, vbuf, 0, 1)
    onward(0, kn, kbuf, 0, 1)
    for jx, jc in arrival[1:]:
        onward(1, v_hbm, vbuf, jx, jc)
    for jx, jc in arrival[1:]:
        onward(0, kn, kbuf, jx, jc)
    for jx, jc in others:
        peer = partner(jx, jc)
        swap(2, qn, qseg, 0, peer, me).start()

    def slab(ref, base, i, part):
        return ref.at[pl.ds(pl.multiple_of(base + i * t + part * sub, sub), sub), :]

    def pass_on(kind, buf, i, part):
        return pltpu.make_async_remote_copy(
            src_ref=slab(buf, seg, i, part), dst_ref=slab(buf, 0, i, part),
            send_sem=h2_s.at[kind, i, part], recv_sem=h2_r.at[kind, i, part],
            device_id={"blk": nxt},
        )

    def relay(step, carry):
        i = nh - 1 - step
        for kind, buf in ((0, kbuf), (1, vbuf)):
            hop(piece(buf, 2 * seg, i), buf, kind, seg, i, h1_s, h1_r).wait_recv()
        for part in reversed(range(NS)):
            for kind, buf in ((0, kbuf), (1, vbuf)):
                pass_on(kind, buf, i, part).start()
        return carry

    lax.fori_loop(0, nh, relay, 0)
    for jx, jc in arrival:
        source = partner(jx, jc)
        swap(2, qn, qseg, 0, source, source).wait_recv()
    own_q.wait()
    own_k.wait()
    own_v.wait()
    loads[2].wait()

    first = start_ref[0] - me * t
    row = lax.broadcasted_iota(jnp.int32, (t, 2 * seg), 0)
    col = lax.broadcasted_iota(jnp.int32, (t, 2 * seg), 1)

    def to_sibling(i, part, c):
        at = (i, pl.ds(part * sub, sub), pl.ds(c * chunk, chunk))
        return pltpu.make_async_remote_copy(
            src_ref=sib_out.at[at], dst_ref=sib_in.at[at],
            send_sem=sib_s.at[i, part, c], recv_sem=sib_r.at[i, part, c],
            device_id={"head": sib},
        )

    def home(x, side, part, c):
        columns = pl.ds(pl.multiple_of(side * half + c * chunk, DH), chunk)
        return rbuf.at[x, pl.ds(part * sub, sub), columns]

    def to_owner(i, part, c, source, owner):
        return pltpu.make_async_remote_copy(
            src_ref=comb.at[i, pl.ds(part * sub, sub), pl.ds(c * chunk, chunk)],
            dst_ref=home(source // 2, source % 2, part, c),
            send_sem=red_s.at[i, part, c], recv_sem=red_r.at[source, part, c],
            device_id={"head": owner},
        )

    def keep(i, part, c):
        return pltpu.make_async_copy(
            comb.at[i, pl.ds(part * sub, sub), pl.ds(c * chunk, chunk)],
            home(chip, core, part, c), keep_sem.at[part, c],
        )

    def block(step, carry):
        i = nh - 1 - step
        rows = pl.ds(pl.multiple_of(i * t, t), t)
        keys = pl.ds(pl.multiple_of(i * t + t, t), 2 * seg)
        oldest = 2 * seg - first - i * t
        allowed = (col <= row + (2 * seg - t)) & (col >= oldest - t)
        held = []
        for h in range(heads):
            at = pl.ds(h * DH, DH)
            s = lax.dot_general(
                qseg[rows, at], kbuf[keys, at], (((1,), (1,)), ((), ())),
                preferred_element_type=jnp.float32,
            )
            s = jnp.where(allowed, s, -1e30)
            peak = jnp.max(s, axis=1, keepdims=True)
            p = jnp.exp2((s - peak) * SCORE)
            held.append((peak, jnp.sum(p, axis=1, keepdims=True)))
            acc[:, at] = jnp.dot(
                p.astype(jnp.bfloat16), vbuf[keys, at], preferred_element_type=jnp.float32
            )

        for part in reversed(range(NS)):
            for kind, buf in ((0, kbuf), (1, vbuf)):
                pass_on(kind, buf, i, part).wait_recv()
            low = part * sub
            many = t - low
            keys = pl.ds(pl.multiple_of(i * t + low, sub), many)
            here = pl.ds(pl.multiple_of(i * t + low, sub), sub)
            age = lax.broadcasted_iota(jnp.int32, (sub, many), 1)
            allowed = (age > lax.broadcasted_iota(jnp.int32, (sub, many), 0)) & (
                age >= oldest - low
            )
            for h in range(heads):
                at = pl.ds(h * DH, DH)
                s = lax.dot_general(
                    qseg[here, at], kbuf[keys, at], (((1,), (1,)), ((), ())),
                    preferred_element_type=jnp.float32,
                )
                s = jnp.where(allowed, s, -1e30)
                peak, total = (value[low:low + sub] for value in held[h])
                top = jnp.maximum(peak, jnp.max(s, axis=1, keepdims=True))
                p = jnp.exp2((s - top) * SCORE)
                fade = jnp.exp2((peak - top) * SCORE)
                total = total * fade + jnp.sum(p, axis=1, keepdims=True)
                o = acc[pl.ds(low, sub), at] * fade + jnp.dot(
                    p.astype(jnp.bfloat16), vbuf[keys, at], preferred_element_type=jnp.float32
                )
                ho[pl.ds(low, sub), at] = (o / total).astype(jnp.bfloat16)

            spot = pl.ds(low, sub)

            def project(side, c):
                at = pl.ds(pl.multiple_of(side * half + c * chunk, DH), chunk)
                return jnp.dot(ho[spot, :], w_ref[:, at], preferred_element_type=jnp.float32)

            for c in range(NC):
                sib_out[i, spot, pl.ds(c * chunk, chunk)] = project(1 - core, c).astype(
                    jnp.bfloat16
                )
                to_sibling(i, part, c).start()
            for c in range(NC):
                at = pl.ds(c * chunk, chunk)
                mine = project(core, c)
                to_sibling(i, part, c).wait_recv()
                both = mine + sib_in[i, spot, at].astype(jnp.float32)
                comb[i, spot, at] = both.astype(jnp.bfloat16)

                @pl.when(me == i)
                def _():
                    keep(i, part, c).start()

                @pl.when(me != i)
                def _():
                    to_owner(i, part, c, me, i).start()

        return carry

    lax.fori_loop(0, nh, block, 0)

    pieces = [(part, c) for part in reversed(range(NS)) for c in range(NC)]
    for part, c in pieces:
        keep(me, part, c).wait()
        for jx, jc in arrival:
            source = partner(jx, jc)
            to_owner(source, part, c, source, source).wait_recv()

    for jx, jc in arrival:
        peer = partner(jx, jc)
        swap(1, v_hbm, vbuf, 2 * seg, peer, me).wait_send()
        swap(0, kn, kbuf, 2 * seg, peer, me).wait_send()
        swap(2, qn, qseg, 0, peer, me).wait_send()
        for part, c in pieces:
            to_owner(peer, part, c, me, peer).wait_send()

    def sent(i, carry):
        for kind, buf in ((0, kbuf), (1, vbuf)):
            hop(piece(buf, 2 * seg, i), buf, kind, seg, i, h1_s, h1_r).wait_send()
            for part in range(NS):
                pass_on(kind, buf, i, part).wait_send()
        for part, c in pieces:
            to_sibling(i, part, c).wait_send()
        return carry

    lax.fori_loop(0, nh, sent, 0)


def line_kernel(
    q_hbm, k_hbm, v_hbm, scale_ref, w_hbm, start_ref, rbuf,
    qin, kin, qn, kn, w_ref, qseg, kbuf, vbuf, gq, xsrc, xin, go, gin, gst, gst_in, turn, near_log,
    acc, own_log, ho, sib_out, sib_in, comb,
    load_sem, loc_sem, keep_sem, a2a_s, a2a_r, qa_s, qa_r, kv_s, kv_r, rl_s, gq_s, gq_r, x_s, x_r,
    go_s, go_r, st_s, st_r, sib_s, sib_r, red_s, red_r,
):
    nh, nb = 4, 4
    t, hd = qin.shape
    cols = hd // nh
    heads = cols // DH
    seg = nh * t
    sub = t // 2
    width = w_ref.shape[1]
    half = width // 2
    chunk = half // NC
    nx = nh // 2
    me = lax.axis_index("head")
    z = lax.axis_index("blk")
    chip = me // 2
    core = me % 2
    sib = chip * 2 + (1 - core)

    def partner(jx, jc):
        return ((chip + jx) % nx) * 2 + (core + jc) % 2

    others = [(jx, 0) for jx in range(1, nx)] + [(jx, 1) for jx in range(nx)]
    arrival = [(jx, jc) for jx in range(nx) for jc in range(2) if jx or jc]

    loads = [
        pltpu.make_async_copy(k_hbm, kin, load_sem.at[0]),
        pltpu.make_async_copy(q_hbm, qin, load_sem.at[1]),
        pltpu.make_async_copy(w_hbm, w_ref, load_sem.at[2]),
    ]
    for copy in loads:
        copy.start()

    barrier = pltpu.get_barrier_semaphore()
    for jx, jc in others:
        pl.semaphore_signal(barrier, inc=1, device_id={"head": partner(jx, jc)})
    for d in range(1, nb):
        pl.semaphore_signal(barrier, inc=1, device_id={"blk": (z + d) % nb})
    pl.semaphore_wait(barrier, nh + nb - 2)

    def group(ref, peer):
        return ref.at[:, pl.ds(pl.multiple_of(peer * cols, DH), cols)]

    def piece(ref, base, index):
        return ref.at[pl.ds(pl.multiple_of(base + index * t, t), t), :]

    def swap(kind, src, dst, base, peer, source):
        return pltpu.make_async_remote_copy(
            src_ref=group(src, peer), dst_ref=piece(dst, base, source),
            send_sem=a2a_s.at[kind, peer], recv_sem=a2a_r.at[kind, source],
            device_id={"head": peer},
        )

    def spot(i, part):
        return ((i % 2) * 2 + part) * t + (i // 2) * sub

    def swap_q(part, peer, source):
        return pltpu.make_async_remote_copy(
            src_ref=qn.at[pl.ds(part * sub, sub), pl.ds(pl.multiple_of(peer * cols, DH), cols)],
            dst_ref=qseg.at[pl.ds(pl.multiple_of(spot(source, part), sub), sub), :],
            send_sem=qa_s.at[part, peer], recv_sem=qa_r.at[part, source],
            device_id={"head": peer},
        )

    def own_half(part):
        return pltpu.make_async_copy(
            qn.at[pl.ds(part * sub, sub), pl.ds(pl.multiple_of(me * cols, DH), cols)],
            qseg.at[pl.ds(pl.multiple_of(spot(me, part), sub), sub), :], loc_sem.at[2 + part],
        )

    far = jnp.where(z == 3, 1, 0)
    hop_base = jnp.where(z == 3, 0, seg)
    hop_to = jnp.where(z == 3, 1, z + 1)

    def hop(src, dst, kind, index):
        return pltpu.make_async_remote_copy(
            src_ref=src, dst_ref=piece(dst, hop_base, index),
            send_sem=kv_s.at[kind, index], recv_sem=kv_r.at[far, kind, index],
            device_id={"blk": hop_to},
        )

    def landed(dst, slot, kind, index):
        return pltpu.make_async_remote_copy(
            src_ref=piece(dst, (1 - slot) * seg, index), dst_ref=piece(dst, (1 - slot) * seg, index),
            send_sem=kv_s.at[kind, index], recv_sem=kv_r.at[slot, kind, index],
            device_id={"blk": hop_to},
        )

    def relay(dst, kind, index):
        return pltpu.make_async_remote_copy(
            src_ref=piece(dst, 0, index), dst_ref=piece(dst, seg, index),
            send_sem=rl_s.at[kind, index], recv_sem=kv_r.at[0, kind, index],
            device_id={"blk": 0},
        )

    def normed(src, dst, peer, factor):
        for h in range(heads):
            at = pl.ds(pl.multiple_of(peer * cols + h * DH, DH), DH)
            x = src[:, at].astype(jnp.float32)
            x = x * lax.rsqrt(jnp.mean(x * x, axis=1, keepdims=True) + 1e-06)
            dst[:, at] = (x * (scale_ref[:, at] * factor)).astype(jnp.bfloat16)

    bufs = (kbuf, vbuf)

    def pass_back(kind, index):
        @pl.when(z == 1)
        def _():
            landed(bufs[kind], 1, kind, index).wait_recv()
            relay(bufs[kind], kind, index).start()

    hop(group(v_hbm, me), vbuf, 1, me).start()
    for jx, jc in others:
        swap(1, v_hbm, vbuf, 2 * seg, partner(jx, jc), me).start()
    own_v = pltpu.make_async_copy(group(v_hbm, me), piece(vbuf, 2 * seg, me), loc_sem.at[1])
    own_v.start()

    loads[0].wait()
    normed(kin, kn, me, 1.0)
    hop(group(kn, me), kbuf, 0, me).start()
    own_k = pltpu.make_async_copy(group(kn, me), piece(kbuf, 2 * seg, me), loc_sem.at[0])
    own_k.start()
    normed(kin, kn, sib, 1.0)
    swap(0, kn, kbuf, 2 * seg, sib, me).start()
    loads[1].wait()
    for jx, jc in others + [(0, 0)]:
        peer = partner(jx, jc)
        normed(qin, qn, peer, SCORE)
        if jx or jc:
            for part in range(2):
                swap_q(part, peer, me).start()
    own_q = [own_half(0), own_half(1)]
    for copy in own_q:
        copy.start()
    for jx, jc in [pair for pair in others if pair[0]]:
        peer = partner(jx, jc)
        normed(kin, kn, peer, 1.0)
        swap(0, kn, kbuf, 2 * seg, peer, me).start()

    def onward(kind, src, buf, jx, jc):
        source = partner(jx, jc)
        swap(kind, src, buf, 2 * seg, source, source).wait_recv()
        hop(piece(buf, 2 * seg, source), buf, kind, source).start()

    onward(1, v_hbm, vbuf, 0, 1)
    onward(0, kn, kbuf, 0, 1)
    pass_back(1, me)
    pass_back(0, me)
    for jx, jc in arrival[1:]:
        onward(1, v_hbm, vbuf, jx, jc)
    pass_back(1, sib)
    pass_back(0, sib)
    first = start_ref[0] - me * t
    both = 2 * t

    def turn_of(step):
        return (step + 2) % nh

    def ask(i):
        return pltpu.make_async_remote_copy(
            src_ref=piece(qseg, 0, i), dst_ref=piece(gq, 0, i),
            send_sem=gq_s.at[i], recv_sem=gq_r.at[i], device_id={"blk": z - 1},
        )

    def ask_low(p):
        return pltpu.make_async_remote_copy(
            src_ref=qseg.at[pl.ds(pl.multiple_of(p * t, t), sub), :],
            dst_ref=gq.at[pl.ds(pl.multiple_of(p * t, t), sub), :],
            send_sem=gq_s.at[p], recv_sem=gq_r.at[p], device_id={"blk": z - 1},
        )

    def cross(n):
        return pltpu.make_async_remote_copy(
            src_ref=piece(xsrc, 0, n), dst_ref=piece(xin, 0, n),
            send_sem=x_s.at[n], recv_sem=x_r.at[n], device_id={"blk": 2},
        )

    for jx, jc in arrival:
        source = partner(jx, jc)
        for part in range(2):
            swap_q(part, source, source).wait_recv()
    for copy in own_q:
        copy.wait()
    own_v.wait()

    def choose(part, buf):
        later = first >= 2 * seg
        for h in range(heads):
            at = pl.ds(h * DH, DH)
            xsrc[pl.ds(part * both, both), at] = jnp.where(
                later, qseg[pl.ds(part * both, both), at],
                buf[pl.ds(2 * seg + both, both), at],
            )
        for n in range(2):
            cross(2 * part + n).start()

    @pl.when(z == 0)
    def _():
        choose(1, vbuf)

    for jx, jc in arrival[1:]:
        onward(0, kn, kbuf, jx, jc)
    own_k.wait()

    @pl.when(z == 0)
    def _():
        choose(0, kbuf)

    for kind in (1, 0):
        for jx, jc in arrival[1:]:
            pass_back(kind, partner(jx, jc))
    loads[2].wait()

    @pl.when(z == 3)
    def _():
        def send(step, carry):
            ask(nh - 1 - step).start()
            return carry

        lax.fori_loop(0, nh, send, 0)

    @pl.when(z == 2)
    def _():
        def send(step, carry):
            ask_low(nh - 1 - step).start()
            return carry

        lax.fori_loop(0, nh, send, 0)

    def prev_in(i, carry):
        for kind in range(2):
            landed(bufs[kind], 0, kind, i).wait_recv()
        return carry

    lax.fori_loop(0, nh, prev_in, 0)

    turn[...] = jnp.zeros_like(turn)
    def ages(count):
        row = lax.broadcasted_iota(jnp.int32, (t, count), 0)
        return row + jnp.where(row >= sub, both - sub, 0)

    def start_of(p):
        return p * sub

    row = ages(2 * seg)
    col = lax.broadcasted_iota(jnp.int32, (t, 2 * seg), 1)

    def weigh(q, keys, values, allowed):
        s = lax.dot_general(
            q, keys, (((1,), (1,)), ((), ())), preferred_element_type=jnp.float32
        )
        s = jnp.where(allowed, s, -1e30)
        peak = jnp.max(s, axis=1, keepdims=True)
        p = jnp.exp2(s - peak).astype(jnp.bfloat16)
        wide = jnp.concatenate([values, jnp.ones(values.shape, jnp.bfloat16)], axis=1)
        out = jnp.dot(p, wide, preferred_element_type=jnp.float32)
        return peak, out[:, DH:], out[:, :DH]

    def partial(q_ref, low, k_ref, k_base, v_ref, v_base, allowed, out_ref):
        size, count = allowed.shape
        rows = pl.ds(pl.multiple_of(low, sub), size)
        keys = pl.ds(k_base, count)
        vals = pl.ds(v_base, count)
        lane = lax.broadcasted_iota(jnp.int32, (size, DH), 1)
        logs = jnp.zeros((size, DH), jnp.float32)
        for h in range(heads):
            at = pl.ds(h * DH, DH)
            peak, total, o = weigh(q_ref[rows, at], k_ref[keys, at], v_ref[vals, at], allowed)
            out_ref[rows, at] = (o / total).astype(out_ref.dtype)
            logs = jnp.where(lane == h, peak + jnp.log(total) * LOG2E, logs)
        return logs

    def older(p):
        return lax.broadcasted_iota(jnp.int32, (t, seg), 1) > ages(seg) + start_of(p)

    def older_low(p, count, skip):
        return lax.broadcasted_iota(jnp.int32, (sub, count), 1) + skip > (
            lax.broadcasted_iota(jnp.int32, (sub, count), 0) + start_of(p)
        )

    def stats(e, p, to):
        return pltpu.make_async_remote_copy(
            src_ref=gst.at[e, p], dst_ref=gst_in.at[p],
            send_sem=st_s.at[e, p], recv_sem=st_r.at[p], device_id={"blk": to},
        )

    def answer(e, p, to, size):
        rows = pl.ds(pl.multiple_of(p * t, t), size)
        return [
            pltpu.make_async_remote_copy(
                src_ref=go.at[e, rows, :], dst_ref=gin.at[rows, :],
                send_sem=go_s.at[e, p], recv_sem=go_r.at[p], device_id={"blk": to},
            ),
            stats(e, p, to),
        ]

    def reply(copies):
        for copy in copies:
            copy.start()

    def help_across(n):
        cross(n).wait_recv()
        logs = partial(xin, n * t, kbuf, 2 * seg, vbuf, 2 * seg, older(n), go.at[1])
        gst[1, n] = logs.T[:heads]
        reply(answer(1, n, 0, t))

    def help_next(p):
        ask(p).wait_recv()
        logs = partial(gq, p * t, kbuf, seg, vbuf, seg, older(p), go.at[0])
        gst[0, p] = logs.T[:heads]
        reply(answer(0, p, 3, t))

    def help_low(p):
        ask_low(p).wait_recv()
        logs = partial(gq, p * t, kbuf, seg, vbuf, seg, older_low(p, seg, 0), go.at[0])
        logs = jnp.concatenate([logs, jnp.zeros((t - sub, DH), jnp.float32)], axis=0)
        gst[0, p] = logs.T[:heads]
        reply(answer(0, p, 2, sub))

    def to_sibling(i, c):
        at = (i, slice(None), pl.ds(c * chunk, chunk))
        return pltpu.make_async_remote_copy(
            src_ref=sib_out.at[at], dst_ref=sib_in.at[at],
            send_sem=sib_s.at[i, c], recv_sem=sib_r.at[i, c],
            device_id={"head": sib},
        )

    def home(x, side, part, c):
        columns = pl.ds(pl.multiple_of(side * half + c * chunk, DH), chunk)
        return rbuf.at[x, pl.ds(pl.multiple_of(part * sub, sub), sub), columns]

    def strip(p, x, c):
        return comb.at[p, pl.ds(x * sub, sub), pl.ds(c * chunk, chunk)]

    def to_owner(p, x, c, source, owner):
        return pltpu.make_async_remote_copy(
            src_ref=strip(p, x, c), dst_ref=home(source // 2, source % 2, p % 2, c),
            send_sem=red_s.at[p, x, c], recv_sem=red_r.at[source, p % 2, c],
            device_id={"head": owner},
        )

    def keep(p, x, c):
        return pltpu.make_async_copy(
            strip(p, x, c), home(chip, core, p % 2, c), keep_sem.at[p % 2, c],
        )

    def order(step):
        return jnp.where(z == 0, turn_of(step), nh - 1 - step)

    def early(step, carry):
        i = order(step)
        rows = pl.ds(pl.multiple_of(i * t, t), t)

        @pl.when(z == 1)
        def _():
            help_low(i)

        @pl.when(z == 2)
        def _():
            help_next(i)
            help_across(turn_of(step))

        allowed = (col <= row + (seg + start_of(i))) & (col >= seg - first)
        own_log[rows, :] = partial(qseg, i * t, kbuf, seg, vbuf, seg, allowed, acc)
        return carry

    lax.fori_loop(0, nh, early, 0)

    def block(step, carry):
        i = order(step)
        rows = pl.ds(pl.multiple_of(i * t, t), t)

        @pl.when(z == 1)
        def _():
            near_log[...] = partial(qseg, i * t, kbuf, 0, vbuf, 0, older(i), gin)

        @pl.when((z == 2) & (i >= 2))
        def _():
            near_log[sub:] = partial(
                qseg, i * t + sub, xin, t, xin, 3 * t, older_low(i, t, t), gin
            )

        @pl.when((z == 2) & (i < 2))
        def _():
            near_log[sub:] = partial(
                qseg, i * t + sub, xin, 0, xin, 2 * t, older_low(i, 2 * t, 0), gin
            )

        @pl.when(z == 2)
        def _():
            for copy in answer(0, i, 2, sub):
                copy.wait_recv()
            turn[:heads] = gst_in[i]
            near_log[:sub] = turn[...].T[:sub]

        @pl.when((z == 0) | (z == 3))
        def _():
            for copy in answer(0, i, 0, t):
                copy.wait_recv()
            turn[:heads] = gst_in[i]
            near_log[...] = turn[...].T

        logs = jnp.where(first >= 2 * seg, near_log[...], -1e30)
        top = jnp.maximum(own_log[rows, :], logs)
        fade = jnp.exp2(own_log[rows, :] - top)
        gain = jnp.exp2(logs - top)
        fade, gain = fade / (fade + gain), gain / (fade + gain)
        for h in range(heads):
            at = pl.ds(h * DH, DH)
            o = acc[rows, at] * fade[:, h:h + 1] + gin[rows, at].astype(
                jnp.float32
            ) * gain[:, h:h + 1]
            ho[:, at] = o.astype(jnp.bfloat16)

        def project(side, c):
            at = pl.ds(pl.multiple_of(side * half + c * chunk, DH), chunk)
            return jnp.dot(ho[...], w_ref[:, at], preferred_element_type=jnp.float32)

        for c in range(NC):
            sib_out[i, :, pl.ds(c * chunk, chunk)] = project(1 - core, c).astype(jnp.bfloat16)
            to_sibling(i, c).start()
        for c in range(NC):
            at = pl.ds(c * chunk, chunk)
            mine = project(core, c)
            to_sibling(i, c).wait_recv()
            whole = mine + sib_in[i, :, at].astype(jnp.float32)
            comb[i, :, at] = whole.astype(jnp.bfloat16)
            for x in range(2):
                owner = i // 2 + 2 * x

                @pl.when(me == owner)
                def _():
                    keep(i, x, c).start()

                @pl.when(me != owner)
                def _():
                    to_owner(i, x, c, me, owner).start()

        return carry

    lax.fori_loop(0, nh, block, 0)

    for part in range(2):
        for c in range(NC):
            keep((me % 2) * 2 + part, 0, c).wait()
            for jx, jc in arrival:
                source = partner(jx, jc)
                to_owner(part, 0, c, source, source).wait_recv()

    for jx, jc in arrival:
        peer = partner(jx, jc)
        swap(1, v_hbm, vbuf, 2 * seg, peer, me).wait_send()
        swap(0, kn, kbuf, 2 * seg, peer, me).wait_send()
        for part in range(2):
            swap_q(part, peer, me).wait_send()

    def sent(i, carry):
        for c in range(NC):
            to_sibling(i, c).wait_send()
            for x in range(2):
                owner = i // 2 + 2 * x

                @pl.when(me != owner)
                def _():
                    to_owner(i, x, c, me, owner).wait_send()

        @pl.when(z == 1)
        def _():
            for kind in range(2):
                relay(bufs[kind], kind, i).wait_send()

        return carry

    lax.fori_loop(0, nh, sent, 0)

    def hop_sent(i, carry):
        for kind in range(2):
            hop(piece(bufs[kind], 2 * seg, i), bufs[kind], kind, i).wait_send()
        return carry

    lax.fori_loop(0, nh, hop_sent, 0)

    @pl.when(z == 0)
    def _():
        for n in range(nh):
            cross(n).wait_send()

    @pl.when(z == 1)
    def _():
        for p in range(nh):
            for copy in answer(0, p, 2, sub):
                copy.wait_send()

    @pl.when(z == 2)
    def _():
        for p in range(nh):
            ask_low(p).wait_send()
        for i in range(nh):
            for copy in answer(0, i, 3, t) + answer(1, i, 0, t):
                copy.wait_send()

    @pl.when(z == 3)
    def _():
        for i in range(nh):
            ask(i).wait_send()


def line_call(queries, keys, values, scale, w_out, stretch_start):
    nh = 4
    t, hd = queries.shape
    cols = hd // nh
    seg = nh * t
    width = w_out.shape[1]
    half = width // 2
    heads = cols // DH
    bf16 = jnp.bfloat16
    f32 = jnp.float32
    dma = pltpu.SemaphoreType.DMA
    anywhere = pl.BlockSpec(memory_space=pltpu.HBM)
    vmem = pl.BlockSpec(memory_space=pltpu.VMEM)
    return pl.pallas_call(
        line_kernel,
        out_shape=pltpu.VMEM((nh // 2, t, width), bf16),
        in_specs=[anywhere, anywhere, anywhere, vmem, anywhere,
                  pl.BlockSpec(memory_space=pltpu.SMEM)],
        out_specs=vmem,
        scratch_shapes=[
            pltpu.VMEM((t, hd), bf16),
            pltpu.VMEM((t, hd), bf16),
            pltpu.VMEM((t, hd), bf16),
            pltpu.VMEM((t, hd), bf16),
            pltpu.VMEM((cols, width), bf16),
            pltpu.VMEM((seg, cols), bf16),
            pltpu.VMEM((3 * seg, cols), bf16),
            pltpu.VMEM((3 * seg, cols), bf16),
            pltpu.VMEM((seg, cols), bf16),
            pltpu.VMEM((seg, cols), bf16),
            pltpu.VMEM((seg, cols), bf16),
            pltpu.VMEM((2, seg, cols), bf16),
            pltpu.VMEM((seg, cols), bf16),
            pltpu.VMEM((2, nh, heads, t), f32),
            pltpu.VMEM((nh, heads, t), f32),
            pltpu.VMEM((DH, t), f32),
            pltpu.VMEM((t, DH), f32),
            pltpu.VMEM((seg, cols), f32),
            pltpu.VMEM((seg, DH), f32),
            pltpu.VMEM((t, cols), bf16),
            pltpu.VMEM((nh, t, half), bf16),
            pltpu.VMEM((nh, t, half), bf16),
            pltpu.VMEM((nh, t, half), bf16),
            dma((3,)),
            dma((4,)),
            dma((2, NC)),
            dma((2, nh)),
            dma((2, nh)),
            dma((2, nh)),
            dma((2, nh)),
            dma((2, nh)),
            dma((2, 2, nh)),
            dma((2, nh)),
            dma((nh,)),
            dma((nh,)),
            dma((nh,)),
            dma((nh,)),
            dma((2, nh)),
            dma((nh,)),
            dma((2, nh)),
            dma((nh,)),
            dma((nh, NC)),
            dma((nh, NC)),
            dma((nh, 2, NC)),
            dma((nh, 2, NC)),
        ],
        compiler_params=pltpu.CompilerParams(
            collective_id=0, has_side_effects=True,
            vmem_limit_bytes=54 * 1024 * 1024,
        ),
    )(queries, keys, values, scale, w_out, stretch_start)


def solution(mesh):
    nh = mesh.shape["head"]
    nb = mesh.shape["blk"]

    def shards(queries, keys, values, scale_qk, w_out, stretch_start):
        if nb == 4 and nh == 4:
            parts = line_call(
                queries, keys, values, scale_qk.reshape(1, -1), w_out, stretch_start
            )
            return jnp.sum(parts.astype(jnp.float32), axis=0).astype(jnp.bfloat16)
        t, hd = queries.shape
        cols = hd // nh
        seg = nh * t
        width = w_out.shape[1]
        half = width // 2
        bf16 = jnp.bfloat16
        dma = pltpu.SemaphoreType.DMA
        anywhere = pl.BlockSpec(memory_space=pltpu.HBM)
        vmem = pl.BlockSpec(memory_space=pltpu.VMEM)
        parts = pl.pallas_call(
            functools.partial(kernel, nh, nb),
            out_shape=pltpu.VMEM((nh // 2, t, width), bf16),
            in_specs=[anywhere, anywhere, anywhere, vmem, anywhere,
                      pl.BlockSpec(memory_space=pltpu.SMEM)],
            out_specs=vmem,
            scratch_shapes=[
                pltpu.VMEM((t, hd), bf16),
                pltpu.VMEM((t, hd), bf16),
                pltpu.VMEM((t, hd), bf16),
                pltpu.VMEM((t, hd), bf16),
                pltpu.VMEM((cols, width), bf16),
                pltpu.VMEM((seg, cols), bf16),
                pltpu.VMEM((3 * seg, cols), bf16),
                pltpu.VMEM((3 * seg, cols), bf16),
                pltpu.VMEM((t, cols), jnp.float32),
                pltpu.VMEM((t, cols), bf16),
                pltpu.VMEM((nh, t, half), bf16),
                pltpu.VMEM((nh, t, half), bf16),
                pltpu.VMEM((nh, t, half), bf16),
                dma((3,)),
                dma((3,)),
                dma((NS, NC)),
                dma((3, nh)),
                dma((3, nh)),
                dma((2, nh)),
                dma((2, nh)),
                dma((2, nh, NS)),
                dma((2, nh, NS)),
                dma((nh, NS, NC)),
                dma((nh, NS, NC)),
                dma((nh, NS, NC)),
                dma((nh, NS, NC)),
            ],
            compiler_params=pltpu.CompilerParams(
                collective_id=0, has_side_effects=True, vmem_limit_bytes=54 * 1024 * 1024
            ),
        )(queries, keys, values, scale_qk.reshape(1, hd), w_out, stretch_start)
        return jnp.sum(parts.astype(jnp.float32), axis=0).astype(bf16)

    return jax.shard_map(
        shards,
        mesh=mesh,
        in_specs=(
            P(("groups", "blk", "head"), None),
            P(("groups", "blk", "head"), None),
            P(("groups", "blk", "head"), None),
            P(),
            P("head", None),
            P(("groups", "blk", "head")),
        ),
        out_specs=P(("groups", "blk", "head"), None),
        check_vma=False,
    )
```

```python
import functools

import jax
import jax.numpy as jnp
from jax import lax
from jax.experimental import pallas as pl
from jax.experimental.pallas import tpu as pltpu
from jax.sharding import PartitionSpec as P

DH = 128
LOG2E = 1.4426950408889634
SCORE = LOG2E / DH**0.5
NC = 2
NS = 2


def kernel(
    nh, nb, q_hbm, k_hbm, v_hbm, scale_ref, w_hbm, start_ref, rbuf,
    qin, kin, qn, kn, w_ref, qseg, kbuf, vbuf, acc, ho, sib_out, sib_in, comb,
    load_sem, loc_sem, keep_sem, a2a_s, a2a_r, h1_s, h1_r, h2_s, h2_r, sib_s, sib_r, red_s, red_r,
):
    t, hd = qin.shape
    cols = hd // nh
    heads = cols // DH
    seg = nh * t
    sub = t // NS
    width = w_ref.shape[1]
    half = width // 2
    chunk = half // NC
    nx = nh // 2
    me = lax.axis_index("head")
    z = lax.axis_index("blk")
    chip = me // 2
    core = me % 2
    sib = chip * 2 + (1 - core)
    nxt = (z + 1) % nb
    prv = (z + nb - 1) % nb

    def partner(jx, jc):
        return ((chip + jx) % nx) * 2 + (core + jc) % 2

    others = [(jx, 0) for jx in range(1, nx)] + [(jx, 1) for jx in range(nx)]
    arrival = [(jx, jc) for jx in range(nx) for jc in range(2) if jx or jc]

    loads = [
        pltpu.make_async_copy(k_hbm, kin, load_sem.at[0]),
        pltpu.make_async_copy(q_hbm, qin, load_sem.at[1]),
        pltpu.make_async_copy(w_hbm, w_ref, load_sem.at[2]),
    ]
    for copy in loads:
        copy.start()

    barrier = pltpu.get_barrier_semaphore()
    for jx, jc in others:
        pl.semaphore_signal(barrier, inc=1, device_id={"head": partner(jx, jc)})
    pl.semaphore_signal(barrier, inc=1, device_id={"blk": nxt})
    pl.semaphore_signal(barrier, inc=1, device_id={"blk": prv})
    pl.semaphore_wait(barrier, nh + 1)

    def group(ref, peer):
        return ref.at[:, pl.ds(pl.multiple_of(peer * cols, DH), cols)]

    def piece(ref, base, index):
        return ref.at[pl.ds(pl.multiple_of(base + index * t, t), t), :]

    def swap(kind, src, dst, base, peer, source):
        return pltpu.make_async_remote_copy(
            src_ref=group(src, peer), dst_ref=piece(dst, base, source),
            send_sem=a2a_s.at[kind, peer], recv_sem=a2a_r.at[kind, source],
            device_id={"head": peer},
        )

    def hop(src, dst, kind, base, index, send, recv):
        return pltpu.make_async_remote_copy(
            src_ref=src, dst_ref=piece(dst, base, index),
            send_sem=send.at[kind, index], recv_sem=recv.at[kind, index],
            device_id={"blk": nxt},
        )

    def normed(src, dst, peer):
        for h in range(heads):
            at = pl.ds(pl.multiple_of(peer * cols + h * DH, DH), DH)
            x = src[:, at].astype(jnp.float32)
            x = x * lax.rsqrt(jnp.mean(x * x, axis=1, keepdims=True) + 1e-06)
            dst[:, at] = (x * scale_ref[:, at]).astype(jnp.bfloat16)

    hop(group(v_hbm, me), vbuf, 1, seg, me, h1_s, h1_r).start()
    for jx, jc in others:
        swap(1, v_hbm, vbuf, 2 * seg, partner(jx, jc), me).start()
    own_v = pltpu.make_async_copy(group(v_hbm, me), piece(vbuf, 2 * seg, me), loc_sem.at[1])
    own_v.start()

    loads[0].wait()
    normed(kin, kn, me)
    hop(group(kn, me), kbuf, 0, seg, me, h1_s, h1_r).start()
    own_k = pltpu.make_async_copy(group(kn, me), piece(kbuf, 2 * seg, me), loc_sem.at[0])
    own_k.start()
    for jx, jc in others:
        peer = partner(jx, jc)
        normed(kin, kn, peer)
        swap(0, kn, kbuf, 2 * seg, peer, me).start()

    loads[1].wait()
    for jx, jc in [(0, 0)] + others:
        normed(qin, qn, partner(jx, jc))
    own_q = pltpu.make_async_copy(group(qn, me), piece(qseg, 0, me), loc_sem.at[2])
    own_q.start()

    def onward(kind, src, buf, jx, jc):
        source = partner(jx, jc)
        swap(kind, src, buf, 2 * seg, source, source).wait_recv()
        hop(piece(buf, 2 * seg, source), buf, kind, seg, source, h1_s, h1_r).start()

    onward(1, v_hbm, vbuf, 0, 1)
    onward(0, kn, kbuf, 0, 1)
    for jx, jc in arrival[1:]:
        onward(1, v_hbm, vbuf, jx, jc)
    for jx, jc in arrival[1:]:
        onward(0, kn, kbuf, jx, jc)
    for jx, jc in others:
        peer = partner(jx, jc)
        swap(2, qn, qseg, 0, peer, me).start()

    def slab(ref, base, i, part):
        return ref.at[pl.ds(pl.multiple_of(base + i * t + part * sub, sub), sub), :]

    def pass_on(kind, buf, i, part):
        return pltpu.make_async_remote_copy(
            src_ref=slab(buf, seg, i, part), dst_ref=slab(buf, 0, i, part),
            send_sem=h2_s.at[kind, i, part], recv_sem=h2_r.at[kind, i, part],
            device_id={"blk": nxt},
        )

    def relay(step, carry):
        i = nh - 1 - step
        for kind, buf in ((0, kbuf), (1, vbuf)):
            hop(piece(buf, 2 * seg, i), buf, kind, seg, i, h1_s, h1_r).wait_recv()
        for part in reversed(range(NS)):
            for kind, buf in ((0, kbuf), (1, vbuf)):
                pass_on(kind, buf, i, part).start()
        return carry

    lax.fori_loop(0, nh, relay, 0)
    for jx, jc in arrival:
        source = partner(jx, jc)
        swap(2, qn, qseg, 0, source, source).wait_recv()
    own_q.wait()
    own_k.wait()
    own_v.wait()
    loads[2].wait()

    first = start_ref[0] - me * t
    row = lax.broadcasted_iota(jnp.int32, (t, 2 * seg), 0)
    col = lax.broadcasted_iota(jnp.int32, (t, 2 * seg), 1)

    def to_sibling(i, part, c):
        at = (i, pl.ds(part * sub, sub), pl.ds(c * chunk, chunk))
        return pltpu.make_async_remote_copy(
            src_ref=sib_out.at[at], dst_ref=sib_in.at[at],
            send_sem=sib_s.at[i, part, c], recv_sem=sib_r.at[i, part, c],
            device_id={"head": sib},
        )

    def home(x, side, part, c):
        columns = pl.ds(pl.multiple_of(side * half + c * chunk, DH), chunk)
        return rbuf.at[x, pl.ds(part * sub, sub), columns]

    def to_owner(i, part, c, source, owner):
        return pltpu.make_async_remote_copy(
            src_ref=comb.at[i, pl.ds(part * sub, sub), pl.ds(c * chunk, chunk)],
            dst_ref=home(source // 2, source % 2, part, c),
            send_sem=red_s.at[i, part, c], recv_sem=red_r.at[source, part, c],
            device_id={"head": owner},
        )

    def keep(i, part, c):
        return pltpu.make_async_copy(
            comb.at[i, pl.ds(part * sub, sub), pl.ds(c * chunk, chunk)],
            home(chip, core, part, c), keep_sem.at[part, c],
        )

    def block(step, carry):
        i = nh - 1 - step
        rows = pl.ds(pl.multiple_of(i * t, t), t)
        keys = pl.ds(pl.multiple_of(i * t + t, t), 2 * seg)
        oldest = 2 * seg - first - i * t
        allowed = (col <= row + (2 * seg - t)) & (col >= oldest - t)
        held = []
        for h in range(heads):
            at = pl.ds(h * DH, DH)
            s = lax.dot_general(
                qseg[rows, at], kbuf[keys, at], (((1,), (1,)), ((), ())),
                preferred_element_type=jnp.float32,
            )
            s = jnp.where(allowed, s, -1e30)
            peak = jnp.max(s, axis=1, keepdims=True)
            p = jnp.exp2((s - peak) * SCORE)
            held.append((peak, jnp.sum(p, axis=1, keepdims=True)))
            acc[:, at] = jnp.dot(
                p.astype(jnp.bfloat16), vbuf[keys, at], preferred_element_type=jnp.float32
            )

        for part in reversed(range(NS)):
            for kind, buf in ((0, kbuf), (1, vbuf)):
                pass_on(kind, buf, i, part).wait_recv()
            low = part * sub
            many = t - low
            keys = pl.ds(pl.multiple_of(i * t + low, sub), many)
            here = pl.ds(pl.multiple_of(i * t + low, sub), sub)
            age = lax.broadcasted_iota(jnp.int32, (sub, many), 1)
            allowed = (age > lax.broadcasted_iota(jnp.int32, (sub, many), 0)) & (
                age >= oldest - low
            )
            for h in range(heads):
                at = pl.ds(h * DH, DH)
                s = lax.dot_general(
                    qseg[here, at], kbuf[keys, at], (((1,), (1,)), ((), ())),
                    preferred_element_type=jnp.float32,
                )
                s = jnp.where(allowed, s, -1e30)
                peak, total = (value[low:low + sub] for value in held[h])
                top = jnp.maximum(peak, jnp.max(s, axis=1, keepdims=True))
                p = jnp.exp2((s - top) * SCORE)
                fade = jnp.exp2((peak - top) * SCORE)
                total = total * fade + jnp.sum(p, axis=1, keepdims=True)
                o = acc[pl.ds(low, sub), at] * fade + jnp.dot(
                    p.astype(jnp.bfloat16), vbuf[keys, at], preferred_element_type=jnp.float32
                )
                ho[pl.ds(low, sub), at] = (o / total).astype(jnp.bfloat16)

            spot = pl.ds(low, sub)

            def project(side, c):
                at = pl.ds(pl.multiple_of(side * half + c * chunk, DH), chunk)
                return jnp.dot(ho[spot, :], w_ref[:, at], preferred_element_type=jnp.float32)

            for c in range(NC):
                sib_out[i, spot, pl.ds(c * chunk, chunk)] = project(1 - core, c).astype(
                    jnp.bfloat16
                )
                to_sibling(i, part, c).start()
            for c in range(NC):
                at = pl.ds(c * chunk, chunk)
                mine = project(core, c)
                to_sibling(i, part, c).wait_recv()
                both = mine + sib_in[i, spot, at].astype(jnp.float32)
                comb[i, spot, at] = both.astype(jnp.bfloat16)

                @pl.when(me == i)
                def _():
                    keep(i, part, c).start()

                @pl.when(me != i)
                def _():
                    to_owner(i, part, c, me, i).start()

        return carry

    lax.fori_loop(0, nh, block, 0)

    pieces = [(part, c) for part in reversed(range(NS)) for c in range(NC)]
    for part, c in pieces:
        keep(me, part, c).wait()
        for jx, jc in arrival:
            source = partner(jx, jc)
            to_owner(source, part, c, source, source).wait_recv()

    for jx, jc in arrival:
        peer = partner(jx, jc)
        swap(1, v_hbm, vbuf, 2 * seg, peer, me).wait_send()
        swap(0, kn, kbuf, 2 * seg, peer, me).wait_send()
        swap(2, qn, qseg, 0, peer, me).wait_send()
        for part, c in pieces:
            to_owner(peer, part, c, me, peer).wait_send()

    def sent(i, carry):
        for kind, buf in ((0, kbuf), (1, vbuf)):
            hop(piece(buf, 2 * seg, i), buf, kind, seg, i, h1_s, h1_r).wait_send()
            for part in range(NS):
                pass_on(kind, buf, i, part).wait_send()
        for part, c in pieces:
            to_sibling(i, part, c).wait_send()
        return carry

    lax.fori_loop(0, nh, sent, 0)


def line_kernel(
    q_hbm, k_hbm, v_hbm, scale_ref, w_hbm, start_ref, rbuf,
    qin, kin, qn, kn, w_ref, qseg, kbuf, vbuf, gq, xsrc, xin, go, gin, gst, gst_in, low_log,
    low_in, turn, wide_turn, far_log, near_log, acc, own_log, acc_prev, prev_log, ho, sib_out, sib_in, comb,
    load_sem, loc_sem, keep_sem, a2a_s, a2a_r, qa_s, qa_r, kv_s, kv_r, rl_s, gq_s, gq_r, x_s, x_r,
    go_s, go_r, st_s, st_r, sib_s, sib_r, red_s, red_r,
):
    nh, nb = 4, 4
    t, hd = qin.shape
    cols = hd // nh
    heads = cols // DH
    seg = nh * t
    sub = t // 2
    width = w_ref.shape[1]
    half = width // 2
    chunk = half // NC
    nx = nh // 2
    me = lax.axis_index("head")
    z = lax.axis_index("blk")
    chip = me // 2
    core = me % 2
    sib = chip * 2 + (1 - core)

    def partner(jx, jc):
        return ((chip + jx) % nx) * 2 + (core + jc) % 2

    others = [(jx, 0) for jx in range(1, nx)] + [(jx, 1) for jx in range(nx)]
    arrival = [(jx, jc) for jx in range(nx) for jc in range(2) if jx or jc]

    loads = [
        pltpu.make_async_copy(k_hbm, kin, load_sem.at[0]),
        pltpu.make_async_copy(q_hbm, qin, load_sem.at[1]),
        pltpu.make_async_copy(w_hbm, w_ref, load_sem.at[2]),
    ]
    for copy in loads:
        copy.start()

    barrier = pltpu.get_barrier_semaphore()
    for jx, jc in others:
        pl.semaphore_signal(barrier, inc=1, device_id={"head": partner(jx, jc)})
    for d in range(1, nb):
        pl.semaphore_signal(barrier, inc=1, device_id={"blk": (z + d) % nb})
    pl.semaphore_wait(barrier, nh + nb - 2)

    def group(ref, peer):
        return ref.at[:, pl.ds(pl.multiple_of(peer * cols, DH), cols)]

    def piece(ref, base, index):
        return ref.at[pl.ds(pl.multiple_of(base + index * t, t), t), :]

    def swap(kind, src, dst, base, peer, source):
        return pltpu.make_async_remote_copy(
            src_ref=group(src, peer), dst_ref=piece(dst, base, source),
            send_sem=a2a_s.at[kind, peer], recv_sem=a2a_r.at[kind, source],
            device_id={"head": peer},
        )

    def spot(i, part):
        return ((i % 2) * 2 + part) * t + (i // 2) * sub

    def swap_q(part, peer, source):
        return pltpu.make_async_remote_copy(
            src_ref=qn.at[pl.ds(part * sub, sub), pl.ds(pl.multiple_of(peer * cols, DH), cols)],
            dst_ref=qseg.at[pl.ds(pl.multiple_of(spot(source, part), sub), sub), :],
            send_sem=qa_s.at[part, peer], recv_sem=qa_r.at[part, source],
            device_id={"head": peer},
        )

    def own_half(part):
        return pltpu.make_async_copy(
            qn.at[pl.ds(part * sub, sub), pl.ds(pl.multiple_of(me * cols, DH), cols)],
            qseg.at[pl.ds(pl.multiple_of(spot(me, part), sub), sub), :], loc_sem.at[2 + part],
        )

    far = jnp.where(z == 3, 1, 0)
    hop_base = jnp.where(z == 3, 0, seg)
    hop_to = jnp.where(z == 3, 1, z + 1)

    def hop(src, dst, kind, index):
        return pltpu.make_async_remote_copy(
            src_ref=src, dst_ref=piece(dst, hop_base, index),
            send_sem=kv_s.at[kind, index], recv_sem=kv_r.at[far, kind, index],
            device_id={"blk": hop_to},
        )

    def landed(dst, slot, kind, index):
        return pltpu.make_async_remote_copy(
            src_ref=piece(dst, (1 - slot) * seg, index), dst_ref=piece(dst, (1 - slot) * seg, index),
            send_sem=kv_s.at[kind, index], recv_sem=kv_r.at[slot, kind, index],
            device_id={"blk": hop_to},
        )

    def relay(dst, kind, index):
        return pltpu.make_async_remote_copy(
            src_ref=piece(dst, 0, index), dst_ref=piece(dst, seg, index),
            send_sem=rl_s.at[kind, index], recv_sem=kv_r.at[0, kind, index],
            device_id={"blk": 0},
        )

    def normed(src, dst, peer, factor):
        for h in range(heads):
            at = pl.ds(pl.multiple_of(peer * cols + h * DH, DH), DH)
            x = src[:, at].astype(jnp.float32)
            x = x * lax.rsqrt(jnp.mean(x * x, axis=1, keepdims=True) + 1e-06)
            dst[:, at] = (x * (scale_ref[:, at] * factor)).astype(jnp.bfloat16)

    bufs = (kbuf, vbuf)

    def pass_back(kind, index):
        @pl.when(z == 1)
        def _():
            landed(bufs[kind], 1, kind, index).wait_recv()
            relay(bufs[kind], kind, index).start()

    hop(group(v_hbm, me), vbuf, 1, me).start()
    for jx, jc in others:
        swap(1, v_hbm, vbuf, 2 * seg, partner(jx, jc), me).start()
    own_v = pltpu.make_async_copy(group(v_hbm, me), piece(vbuf, 2 * seg, me), loc_sem.at[1])
    own_v.start()

    loads[0].wait()
    normed(kin, kn, me, 1.0)
    hop(group(kn, me), kbuf, 0, me).start()
    own_k = pltpu.make_async_copy(group(kn, me), piece(kbuf, 2 * seg, me), loc_sem.at[0])
    own_k.start()
    for jx, jc in others:
        peer = partner(jx, jc)
        normed(kin, kn, peer, 1.0)
        swap(0, kn, kbuf, 2 * seg, peer, me).start()
    loads[1].wait()
    for jx, jc in others + [(0, 0)]:
        peer = partner(jx, jc)
        normed(qin, qn, peer, SCORE)
        if jx or jc:
            for part in range(2):
                swap_q(part, peer, me).start()
    own_q = [own_half(0), own_half(1)]
    for copy in own_q:
        copy.start()

    def onward(kind, src, buf, jx, jc):
        source = partner(jx, jc)
        swap(kind, src, buf, 2 * seg, source, source).wait_recv()
        hop(piece(buf, 2 * seg, source), buf, kind, source).start()

    onward(1, v_hbm, vbuf, 0, 1)
    onward(0, kn, kbuf, 0, 1)
    pass_back(1, me)
    pass_back(0, me)
    for jx, jc in arrival[1:]:
        onward(1, v_hbm, vbuf, jx, jc)
    pass_back(1, sib)
    pass_back(0, sib)
    first = start_ref[0] - me * t
    both = 2 * t

    def ask(p):
        return pltpu.make_async_remote_copy(
            src_ref=piece(qseg, 0, p), dst_ref=piece(gq, 0, p),
            send_sem=gq_s.at[p], recv_sem=gq_r.at[p], device_id={"blk": z - 1},
        )

    def ask_low(p):
        return pltpu.make_async_remote_copy(
            src_ref=qseg.at[pl.ds(pl.multiple_of(p * t, t), sub), :],
            dst_ref=gq.at[pl.ds(pl.multiple_of(p * sub, sub), sub), :],
            send_sem=gq_s.at[p], recv_sem=gq_r.at[p], device_id={"blk": z - 1},
        )

    def cross(n):
        return pltpu.make_async_remote_copy(
            src_ref=piece(xsrc, 0, n), dst_ref=piece(xin, 0, n),
            send_sem=x_s.at[n], recv_sem=x_r.at[n], device_id={"blk": 2},
        )

    for jx, jc in arrival[1:]:
        source = partner(jx, jc)
        swap(0, kn, kbuf, 2 * seg, source, source).wait_recv()

        @pl.when(z != 0)
        def _():
            hop(piece(kbuf, 2 * seg, source), kbuf, 0, source).start()

    for jx, jc in arrival:
        source = partner(jx, jc)
        for part in range(2):
            swap_q(part, source, source).wait_recv()
    for copy in own_q:
        copy.wait()
    own_v.wait()
    own_k.wait()

    def choose(pair):
        later = first >= 2 * seg
        for part, buf in ((0, kbuf), (1, vbuf)):
            n = 2 * pair + part
            for h in range(heads):
                at = pl.ds(h * DH, DH)
                xsrc[pl.ds(n * t, t), at] = jnp.where(
                    later, qseg[pl.ds(n * t, t), at],
                    buf[pl.ds(2 * seg + (3 - pair) * t, t), at],
                )
            cross(n).start()

    @pl.when(z == 0)
    def _():
        choose(0)
        for jx, jc in arrival[1:]:
            source = partner(jx, jc)
            hop(piece(kbuf, 2 * seg, source), kbuf, 0, source).start()
        choose(1)

    for jx, jc in arrival[1:]:
        pass_back(1, partner(jx, jc))

    @pl.when(z == 3)
    def _():
        def send(step, carry):
            ask(nh - 1 - step).start()
            return carry

        lax.fori_loop(0, nh, send, 0)

    @pl.when(z == 2)
    def _():
        def send(step, carry):
            ask_low(nh - 1 - step).start()
            return carry

        lax.fori_loop(0, nh, send, 0)

    def weigh(q, keys, values, allowed):
        s = lax.dot_general(
            q, keys, (((1,), (1,)), ((), ())), preferred_element_type=jnp.float32
        )
        if allowed is not None:
            s = jnp.where(allowed, s, -1e30)
        peak = jnp.max(s, axis=1, keepdims=True)
        p = jnp.exp2(s - peak).astype(jnp.bfloat16)
        wide = jnp.concatenate([values, jnp.ones(values.shape, jnp.bfloat16)], axis=1)
        out = jnp.dot(p, wide, preferred_element_type=jnp.float32)
        return peak, out[:, DH:], out[:, :DH]

    def partial(size, q_of, k_of, v_of, allowed, put):
        lane = lax.broadcasted_iota(jnp.int32, (size, DH), 1)
        logs = jnp.zeros((size, DH), jnp.float32)
        for h in range(heads):
            at = pl.ds(h * DH, DH)
            peak, total, o = weigh(q_of(at), k_of(at), v_of(at), allowed)
            put(at, o / total)
            logs = jnp.where(lane == h, peak + jnp.log(total) * LOG2E, logs)
        return logs

    def cut(ref, base, size):
        rows = pl.ds(pl.multiple_of(base, sub), size)
        return lambda at: ref[rows, at]

    def into(ref, base, size):
        rows = pl.ds(pl.multiple_of(base, sub), size)

        def put(at, value):
            ref[rows, at] = value.astype(ref.dtype)

        return put

    def pair_rows(pair):
        return pl.ds(pl.multiple_of(pair * both, both), both)

    def ages(pair):
        r = lax.broadcasted_iota(jnp.int32, (both, seg), 0)
        upper = jnp.where(r < t + sub, r - sub, r + both - t)
        return jnp.where(r < sub, r, jnp.where(r < t, r + both - sub, upper)) + pair * t

    col = lax.broadcasted_iota(jnp.int32, (both, seg), 1)

    def own_part(pair, carry):
        own_log[pair_rows(pair), :] = partial(
            both, cut(qseg, pair * both, both), cut(kbuf, 2 * seg, seg), cut(vbuf, 2 * seg, seg),
            col <= ages(pair), into(acc, pair * both, both),
        )
        return carry

    lax.fori_loop(0, 2, own_part, 0)

    for jx, jc in arrival[1:]:
        pass_back(0, partner(jx, jc))
    loads[2].wait()

    def stats(e, p, to):
        return pltpu.make_async_remote_copy(
            src_ref=gst.at[e, p], dst_ref=gst_in.at[p],
            send_sem=st_s.at[e, p], recv_sem=st_r.at[p], device_id={"blk": to},
        )

    def answer(e, p, to):
        return [
            pltpu.make_async_remote_copy(
                src_ref=piece(go.at[e], 0, p), dst_ref=piece(gin, 0, p),
                send_sem=go_s.at[e, p], recv_sem=go_r.at[p], device_id={"blk": to},
            ),
            stats(e, p, to),
        ]

    def low_answer(p):
        return pltpu.make_async_remote_copy(
            src_ref=go.at[0, pl.ds(pl.multiple_of(p * sub, sub), sub), :],
            dst_ref=gin.at[pl.ds(pl.multiple_of(p * t, t), sub), :],
            send_sem=go_s.at[0, p], recv_sem=go_r.at[p], device_id={"blk": 2},
        )

    low_stats = pltpu.make_async_remote_copy(
        src_ref=low_log, dst_ref=low_in,
        send_sem=st_s.at[0, 0], recv_sem=st_r.at[0], device_id={"blk": 2},
    )

    def serve(e, pair, q_ref, base, to):
        logs = partial(
            both, cut(q_ref, pair * both, both), cut(kbuf, base, seg), cut(vbuf, base, seg),
            col > ages(pair), into(go.at[e], pair * both, both),
        ).T[:heads]
        for n in range(2):
            gst[e, 2 * pair + n] = logs[:, n * t:(n + 1) * t]
        for n in (1, 0):
            for copy in answer(e, 2 * pair + n, to):
                copy.start()

    def help_across(pair):
        for n in range(2):
            cross(2 * pair + n).wait_recv()
        serve(1, pair, xin, 2 * seg, 0)

    def help_next(pair):
        for n in range(2):
            ask(2 * pair + n).wait_recv()
        serve(0, pair, gq, seg, 3)

    @pl.when(z == 2)
    def _():
        help_across(0)

    def prev_in(i, carry):
        for kind in range(2):
            landed(bufs[kind], 0, kind, i).wait_recv()
        return carry

    lax.fori_loop(0, nh, prev_in, 0)

    turn[...] = jnp.zeros_like(turn)
    wide_turn[...] = jnp.zeros_like(wide_turn)

    @pl.when(z == 1)
    def _():
        for p in range(nh):
            ask_low(p).wait_recv()
        low_log[...] = partial(
            both, cut(gq, 0, both), cut(kbuf, seg, seg), cut(vbuf, seg, seg),
            col > lax.broadcasted_iota(jnp.int32, (both, seg), 0), into(go.at[0], 0, both),
        ).T[:heads]
        low_stats.start()
        for p in reversed(range(nh)):
            low_answer(p).start()

    def to_sibling(i, c):
        at = (i, slice(None), pl.ds(c * chunk, chunk))
        return pltpu.make_async_remote_copy(
            src_ref=sib_out.at[at], dst_ref=sib_in.at[at],
            send_sem=sib_s.at[i, c], recv_sem=sib_r.at[i, c],
            device_id={"head": sib},
        )

    def home(x, side, part, c):
        columns = pl.ds(pl.multiple_of(side * half + c * chunk, DH), chunk)
        return rbuf.at[x, pl.ds(pl.multiple_of(part * sub, sub), sub), columns]

    def strip(p, x, c):
        return comb.at[p, pl.ds(x * sub, sub), pl.ds(c * chunk, chunk)]

    def to_owner(p, x, c, source, owner):
        return pltpu.make_async_remote_copy(
            src_ref=strip(p, x, c), dst_ref=home(source // 2, source % 2, p % 2, c),
            send_sem=red_s.at[p, x, c], recv_sem=red_r.at[source, p % 2, c],
            device_id={"head": owner},
        )

    def keep(p, x, c):
        return pltpu.make_async_copy(
            strip(p, x, c), home(chip, core, p % 2, c), keep_sem.at[p % 2, c],
        )

    def near_part(pair, count):
        rows = [pl.ds((2 * pair + n) * t + sub, sub) for n in range(2)]

        def newest(first_slot):
            def of(at):
                last = xin[pl.ds(first_slot * t, t), at]
                if count == t:
                    return last
                return jnp.concatenate([xin[pl.ds((first_slot + 2) * t, t), at], last], axis=0)

            return of

        def put(at, value):
            for n in range(2):
                gin[rows[n], at] = value[n * sub:(n + 1) * sub].astype(gin.dtype)

        far_log[pl.ds(pair * t, t), :] = partial(
            t, lambda at: jnp.concatenate([qseg[rows[0], at], qseg[rows[1], at]], axis=0),
            newest(0), newest(1),
            lax.broadcasted_iota(jnp.int32, (t, count), 1)
            > lax.broadcasted_iota(jnp.int32, (t, count), 0), put,
        )

    def turn_pair(step):
        pair = jnp.where(z == 0, step, 1 - step)
        prev_log[pair_rows(pair), :] = partial(
            both, cut(qseg, pair * both, both), cut(kbuf, seg, seg), cut(vbuf, seg, seg), None,
            into(acc_prev, pair * both, both),
        )

        @pl.when(z == 1)
        def _():
            far_log[pair_rows(pair), :] = partial(
                both, cut(qseg, pair * both, both), cut(kbuf, 0, seg), cut(vbuf, 0, seg),
                col > ages(pair), into(gin, pair * both, both),
            )

        @pl.when((z == 2) & (step == 0))
        def _():
            help_next(1)
            near_part(1, t)
            help_next(0)
            help_across(1)

        @pl.when((z == 2) & (step == 1))
        def _():
            near_part(0, both)

    def block(step, carry):
        @pl.when(step % 2 == 0)
        def _():
            turn_pair(step // 2)

        i = jnp.where(z == 0, step // 2 * 2 + 1 - step % 2, nh - 1 - step)
        rows = pl.ds(pl.multiple_of(i * t, t), t)

        @pl.when(z == 1)
        def _():
            near_log[...] = far_log[rows, :]

        @pl.when((z == 2) & (step == 0))
        def _():
            low_stats.wait_recv()
            wide_turn[:heads] = low_in[...]
            far_log[both:] = wide_turn[...].T

        @pl.when(z == 2)
        def _():
            low_answer(i).wait_recv()
            near_log[:sub] = far_log[pl.ds(pl.multiple_of(both + i * sub, sub), sub), :]
            near_log[sub:] = far_log[pl.ds(pl.multiple_of(i * sub, sub), sub), :]

        @pl.when((z == 0) | (z == 3))
        def _():
            for copy in answer(0, i, 0):
                copy.wait_recv()
            turn[:heads] = gst_in[i]
            near_log[...] = turn[...].T

        own = own_log[rows, :]
        before = jnp.where(first >= seg, prev_log[rows, :], -1e30)
        logs = jnp.where(first >= 2 * seg, near_log[...], -1e30)
        top = jnp.maximum(jnp.maximum(own, before), logs)
        own, before, logs = jnp.exp2(own - top), jnp.exp2(before - top), jnp.exp2(logs - top)
        share = 1.0 / (own + before + logs)
        own, before, logs = own * share, before * share, logs * share
        for h in range(heads):
            at = pl.ds(h * DH, DH)
            o = acc[rows, at] * own[:, h:h + 1] + acc_prev[rows, at] * before[:, h:h + 1]
            o = o + gin[rows, at].astype(jnp.float32) * logs[:, h:h + 1]
            ho[:, at] = o.astype(jnp.bfloat16)

        def project(side, c):
            at = pl.ds(pl.multiple_of(side * half + c * chunk, DH), chunk)
            return jnp.dot(ho[...], w_ref[:, at], preferred_element_type=jnp.float32)

        for c in range(NC):
            sib_out[i, :, pl.ds(c * chunk, chunk)] = project(1 - core, c).astype(jnp.bfloat16)
            to_sibling(i, c).start()
        for c in range(NC):
            at = pl.ds(c * chunk, chunk)
            mine = project(core, c)
            to_sibling(i, c).wait_recv()
            whole = mine + sib_in[i, :, at].astype(jnp.float32)
            comb[i, :, at] = whole.astype(jnp.bfloat16)
            for x in range(2):
                owner = i // 2 + 2 * x

                @pl.when(me == owner)
                def _():
                    keep(i, x, c).start()

                @pl.when(me != owner)
                def _():
                    to_owner(i, x, c, me, owner).start()

        return carry

    lax.fori_loop(0, nh, block, 0)

    for part in range(2):
        for c in range(NC):
            keep((me % 2) * 2 + part, 0, c).wait()
            for jx, jc in arrival:
                source = partner(jx, jc)
                to_owner(part, 0, c, source, source).wait_recv()

    for jx, jc in arrival:
        peer = partner(jx, jc)
        swap(1, v_hbm, vbuf, 2 * seg, peer, me).wait_send()
        swap(0, kn, kbuf, 2 * seg, peer, me).wait_send()
        for part in range(2):
            swap_q(part, peer, me).wait_send()

    def sent(i, carry):
        for c in range(NC):
            to_sibling(i, c).wait_send()
            for x in range(2):
                owner = i // 2 + 2 * x

                @pl.when(me != owner)
                def _():
                    to_owner(i, x, c, me, owner).wait_send()

        @pl.when(z == 1)
        def _():
            for kind in range(2):
                relay(bufs[kind], kind, i).wait_send()

        return carry

    lax.fori_loop(0, nh, sent, 0)

    def hop_sent(i, carry):
        for kind in range(2):
            hop(piece(bufs[kind], 2 * seg, i), bufs[kind], kind, i).wait_send()
        return carry

    lax.fori_loop(0, nh, hop_sent, 0)

    @pl.when(z == 0)
    def _():
        for n in range(nh):
            cross(n).wait_send()

    @pl.when(z == 1)
    def _():
        low_stats.wait_send()
        for p in range(nh):
            low_answer(p).wait_send()

    @pl.when(z == 2)
    def _():
        for p in range(nh):
            ask_low(p).wait_send()
        for i in range(nh):
            for copy in answer(0, i, 3) + answer(1, i, 0):
                copy.wait_send()

    @pl.when(z == 3)
    def _():
        for i in range(nh):
            ask(i).wait_send()


def line_call(queries, keys, values, scale, w_out, stretch_start):
    nh = 4
    t, hd = queries.shape
    cols = hd // nh
    seg = nh * t
    width = w_out.shape[1]
    half = width // 2
    heads = cols // DH
    bf16 = jnp.bfloat16
    f32 = jnp.float32
    dma = pltpu.SemaphoreType.DMA
    anywhere = pl.BlockSpec(memory_space=pltpu.HBM)
    vmem = pl.BlockSpec(memory_space=pltpu.VMEM)
    return pl.pallas_call(
        line_kernel,
        out_shape=pltpu.VMEM((nh // 2, t, width), bf16),
        in_specs=[anywhere, anywhere, anywhere, vmem, anywhere,
                  pl.BlockSpec(memory_space=pltpu.SMEM)],
        out_specs=vmem,
        scratch_shapes=[
            pltpu.VMEM((t, hd), bf16),
            pltpu.VMEM((t, hd), bf16),
            pltpu.VMEM((t, hd), bf16),
            pltpu.VMEM((t, hd), bf16),
            pltpu.VMEM((cols, width), bf16),
            pltpu.VMEM((seg, cols), bf16),
            pltpu.VMEM((3 * seg, cols), bf16),
            pltpu.VMEM((3 * seg, cols), bf16),
            pltpu.VMEM((seg, cols), bf16),
            pltpu.VMEM((seg, cols), bf16),
            pltpu.VMEM((seg, cols), bf16),
            pltpu.VMEM((2, seg, cols), bf16),
            pltpu.VMEM((seg, cols), bf16),
            pltpu.VMEM((2, nh, heads, t), f32),
            pltpu.VMEM((nh, heads, t), f32),
            pltpu.VMEM((heads, 2 * t), f32),
            pltpu.VMEM((heads, 2 * t), f32),
            pltpu.VMEM((DH, t), f32),
            pltpu.VMEM((DH, 2 * t), f32),
            pltpu.VMEM((seg, DH), f32),
            pltpu.VMEM((t, DH), f32),
            pltpu.VMEM((seg, cols), f32),
            pltpu.VMEM((seg, DH), f32),
            pltpu.VMEM((seg, cols), f32),
            pltpu.VMEM((seg, DH), f32),
            pltpu.VMEM((t, cols), bf16),
            pltpu.VMEM((nh, t, half), bf16),
            pltpu.VMEM((nh, t, half), bf16),
            pltpu.VMEM((nh, t, half), bf16),
            dma((3,)),
            dma((4,)),
            dma((2, NC)),
            dma((2, nh)),
            dma((2, nh)),
            dma((2, nh)),
            dma((2, nh)),
            dma((2, nh)),
            dma((2, 2, nh)),
            dma((2, nh)),
            dma((nh,)),
            dma((nh,)),
            dma((nh,)),
            dma((nh,)),
            dma((2, nh)),
            dma((nh,)),
            dma((2, nh)),
            dma((nh,)),
            dma((nh, NC)),
            dma((nh, NC)),
            dma((nh, 2, NC)),
            dma((nh, 2, NC)),
        ],
        compiler_params=pltpu.CompilerParams(
            collective_id=0, has_side_effects=True,
            vmem_limit_bytes=54 * 1024 * 1024,
        ),
    )(queries, keys, values, scale, w_out, stretch_start)


def solution(mesh):
    nh = mesh.shape["head"]
    nb = mesh.shape["blk"]

    def shards(queries, keys, values, scale_qk, w_out, stretch_start):
        if nb == 4 and nh == 4:
            parts = line_call(
                queries, keys, values, scale_qk.reshape(1, -1), w_out, stretch_start
            )
            return jnp.sum(parts.astype(jnp.float32), axis=0).astype(jnp.bfloat16)
        t, hd = queries.shape
        cols = hd // nh
        seg = nh * t
        width = w_out.shape[1]
        half = width // 2
        bf16 = jnp.bfloat16
        dma = pltpu.SemaphoreType.DMA
        anywhere = pl.BlockSpec(memory_space=pltpu.HBM)
        vmem = pl.BlockSpec(memory_space=pltpu.VMEM)
        parts = pl.pallas_call(
            functools.partial(kernel, nh, nb),
            out_shape=pltpu.VMEM((nh // 2, t, width), bf16),
            in_specs=[anywhere, anywhere, anywhere, vmem, anywhere,
                      pl.BlockSpec(memory_space=pltpu.SMEM)],
            out_specs=vmem,
            scratch_shapes=[
                pltpu.VMEM((t, hd), bf16),
                pltpu.VMEM((t, hd), bf16),
                pltpu.VMEM((t, hd), bf16),
                pltpu.VMEM((t, hd), bf16),
                pltpu.VMEM((cols, width), bf16),
                pltpu.VMEM((seg, cols), bf16),
                pltpu.VMEM((3 * seg, cols), bf16),
                pltpu.VMEM((3 * seg, cols), bf16),
                pltpu.VMEM((t, cols), jnp.float32),
                pltpu.VMEM((t, cols), bf16),
                pltpu.VMEM((nh, t, half), bf16),
                pltpu.VMEM((nh, t, half), bf16),
                pltpu.VMEM((nh, t, half), bf16),
                dma((3,)),
                dma((3,)),
                dma((NS, NC)),
                dma((3, nh)),
                dma((3, nh)),
                dma((2, nh)),
                dma((2, nh)),
                dma((2, nh, NS)),
                dma((2, nh, NS)),
                dma((nh, NS, NC)),
                dma((nh, NS, NC)),
                dma((nh, NS, NC)),
                dma((nh, NS, NC)),
            ],
            compiler_params=pltpu.CompilerParams(
                collective_id=0, has_side_effects=True, vmem_limit_bytes=54 * 1024 * 1024
            ),
        )(queries, keys, values, scale_qk.reshape(1, hd), w_out, stretch_start)
        return jnp.sum(parts.astype(jnp.float32), axis=0).astype(bf16)

    return jax.shard_map(
        shards,
        mesh=mesh,
        in_specs=(
            P(("groups", "blk", "head"), None),
            P(("groups", "blk", "head"), None),
            P(("groups", "blk", "head"), None),
            P(),
            P("head", None),
            P(("groups", "blk", "head")),
        ),
        out_specs=P(("groups", "blk", "head"), None),
        check_vma=False,
    )
```

```python
import functools

import jax
import jax.numpy as jnp
from jax import lax
from jax.experimental import pallas as pl
from jax.experimental.pallas import tpu as pltpu
from jax.sharding import PartitionSpec as P

DH = 128
LOG2E = 1.4426950408889634
SCORE = LOG2E / DH**0.5
NC = 2
NS = 2


def kernel(
    nh, nb, q_hbm, k_hbm, v_hbm, scale_ref, w_hbm, start_ref, rbuf,
    qin, kin, qn, kn, w_ref, qseg, kbuf, vbuf, acc, ho, sib_out, sib_in, comb,
    load_sem, loc_sem, keep_sem, a2a_s, a2a_r, h1_s, h1_r, h2_s, h2_r, sib_s, sib_r, red_s, red_r,
):
    t, hd = qin.shape
    cols = hd // nh
    heads = cols // DH
    seg = nh * t
    sub = t // NS
    width = w_ref.shape[1]
    half = width // 2
    chunk = half // NC
    nx = nh // 2
    me = lax.axis_index("head")
    z = lax.axis_index("blk")
    chip = me // 2
    core = me % 2
    sib = chip * 2 + (1 - core)
    nxt = (z + 1) % nb
    prv = (z + nb - 1) % nb

    def partner(jx, jc):
        return ((chip + jx) % nx) * 2 + (core + jc) % 2

    others = [(jx, 0) for jx in range(1, nx)] + [(jx, 1) for jx in range(nx)]
    arrival = [(jx, jc) for jx in range(nx) for jc in range(2) if jx or jc]

    loads = [
        pltpu.make_async_copy(k_hbm, kin, load_sem.at[0]),
        pltpu.make_async_copy(q_hbm, qin, load_sem.at[1]),
        pltpu.make_async_copy(w_hbm, w_ref, load_sem.at[2]),
    ]
    for copy in loads:
        copy.start()

    barrier = pltpu.get_barrier_semaphore()
    for jx, jc in others:
        pl.semaphore_signal(barrier, inc=1, device_id={"head": partner(jx, jc)})
    pl.semaphore_signal(barrier, inc=1, device_id={"blk": nxt})
    pl.semaphore_signal(barrier, inc=1, device_id={"blk": prv})
    pl.semaphore_wait(barrier, nh + 1)

    def group(ref, peer):
        return ref.at[:, pl.ds(pl.multiple_of(peer * cols, DH), cols)]

    def piece(ref, base, index):
        return ref.at[pl.ds(pl.multiple_of(base + index * t, t), t), :]

    def swap(kind, src, dst, base, peer, source):
        return pltpu.make_async_remote_copy(
            src_ref=group(src, peer), dst_ref=piece(dst, base, source),
            send_sem=a2a_s.at[kind, peer], recv_sem=a2a_r.at[kind, source],
            device_id={"head": peer},
        )

    def hop(src, dst, kind, base, index, send, recv):
        return pltpu.make_async_remote_copy(
            src_ref=src, dst_ref=piece(dst, base, index),
            send_sem=send.at[kind, index], recv_sem=recv.at[kind, index],
            device_id={"blk": nxt},
        )

    def normed(src, dst, peer):
        for h in range(heads):
            at = pl.ds(pl.multiple_of(peer * cols + h * DH, DH), DH)
            x = src[:, at].astype(jnp.float32)
            x = x * lax.rsqrt(jnp.mean(x * x, axis=1, keepdims=True) + 1e-06)
            dst[:, at] = (x * scale_ref[:, at]).astype(jnp.bfloat16)

    hop(group(v_hbm, me), vbuf, 1, seg, me, h1_s, h1_r).start()
    for jx, jc in others:
        swap(1, v_hbm, vbuf, 2 * seg, partner(jx, jc), me).start()
    own_v = pltpu.make_async_copy(group(v_hbm, me), piece(vbuf, 2 * seg, me), loc_sem.at[1])
    own_v.start()

    loads[0].wait()
    normed(kin, kn, me)
    hop(group(kn, me), kbuf, 0, seg, me, h1_s, h1_r).start()
    own_k = pltpu.make_async_copy(group(kn, me), piece(kbuf, 2 * seg, me), loc_sem.at[0])
    own_k.start()
    for jx, jc in others:
        peer = partner(jx, jc)
        normed(kin, kn, peer)
        swap(0, kn, kbuf, 2 * seg, peer, me).start()

    loads[1].wait()
    for jx, jc in [(0, 0)] + others:
        normed(qin, qn, partner(jx, jc))
    own_q = pltpu.make_async_copy(group(qn, me), piece(qseg, 0, me), loc_sem.at[2])
    own_q.start()

    def onward(kind, src, buf, jx, jc):
        source = partner(jx, jc)
        swap(kind, src, buf, 2 * seg, source, source).wait_recv()
        hop(piece(buf, 2 * seg, source), buf, kind, seg, source, h1_s, h1_r).start()

    onward(1, v_hbm, vbuf, 0, 1)
    onward(0, kn, kbuf, 0, 1)
    for jx, jc in arrival[1:]:
        onward(1, v_hbm, vbuf, jx, jc)
    for jx, jc in arrival[1:]:
        onward(0, kn, kbuf, jx, jc)
    for jx, jc in others:
        peer = partner(jx, jc)
        swap(2, qn, qseg, 0, peer, me).start()

    def slab(ref, base, i, part):
        return ref.at[pl.ds(pl.multiple_of(base + i * t + part * sub, sub), sub), :]

    def pass_on(kind, buf, i, part):
        return pltpu.make_async_remote_copy(
            src_ref=slab(buf, seg, i, part), dst_ref=slab(buf, 0, i, part),
            send_sem=h2_s.at[kind, i, part], recv_sem=h2_r.at[kind, i, part],
            device_id={"blk": nxt},
        )

    def relay(step, carry):
        i = nh - 1 - step
        for kind, buf in ((0, kbuf), (1, vbuf)):
            hop(piece(buf, 2 * seg, i), buf, kind, seg, i, h1_s, h1_r).wait_recv()
        for part in reversed(range(NS)):
            for kind, buf in ((0, kbuf), (1, vbuf)):
                pass_on(kind, buf, i, part).start()
        return carry

    lax.fori_loop(0, nh, relay, 0)
    for jx, jc in arrival:
        source = partner(jx, jc)
        swap(2, qn, qseg, 0, source, source).wait_recv()
    own_q.wait()
    own_k.wait()
    own_v.wait()
    loads[2].wait()

    first = start_ref[0] - me * t
    row = lax.broadcasted_iota(jnp.int32, (t, 2 * seg), 0)
    col = lax.broadcasted_iota(jnp.int32, (t, 2 * seg), 1)

    def to_sibling(i, part, c):
        at = (i, pl.ds(part * sub, sub), pl.ds(c * chunk, chunk))
        return pltpu.make_async_remote_copy(
            src_ref=sib_out.at[at], dst_ref=sib_in.at[at],
            send_sem=sib_s.at[i, part, c], recv_sem=sib_r.at[i, part, c],
            device_id={"head": sib},
        )

    def home(x, side, part, c):
        columns = pl.ds(pl.multiple_of(side * half + c * chunk, DH), chunk)
        return rbuf.at[x, pl.ds(part * sub, sub), columns]

    def to_owner(i, part, c, source, owner):
        return pltpu.make_async_remote_copy(
            src_ref=comb.at[i, pl.ds(part * sub, sub), pl.ds(c * chunk, chunk)],
            dst_ref=home(source // 2, source % 2, part, c),
            send_sem=red_s.at[i, part, c], recv_sem=red_r.at[source, part, c],
            device_id={"head": owner},
        )

    def keep(i, part, c):
        return pltpu.make_async_copy(
            comb.at[i, pl.ds(part * sub, sub), pl.ds(c * chunk, chunk)],
            home(chip, core, part, c), keep_sem.at[part, c],
        )

    def block(step, carry):
        i = nh - 1 - step
        rows = pl.ds(pl.multiple_of(i * t, t), t)
        keys = pl.ds(pl.multiple_of(i * t + t, t), 2 * seg)
        oldest = 2 * seg - first - i * t
        allowed = (col <= row + (2 * seg - t)) & (col >= oldest - t)
        held = []
        for h in range(heads):
            at = pl.ds(h * DH, DH)
            s = lax.dot_general(
                qseg[rows, at], kbuf[keys, at], (((1,), (1,)), ((), ())),
                preferred_element_type=jnp.float32,
            )
            s = jnp.where(allowed, s, -1e30)
            peak = jnp.max(s, axis=1, keepdims=True)
            p = jnp.exp2((s - peak) * SCORE)
            held.append((peak, jnp.sum(p, axis=1, keepdims=True)))
            acc[:, at] = jnp.dot(
                p.astype(jnp.bfloat16), vbuf[keys, at], preferred_element_type=jnp.float32
            )

        for part in reversed(range(NS)):
            for kind, buf in ((0, kbuf), (1, vbuf)):
                pass_on(kind, buf, i, part).wait_recv()
            low = part * sub
            many = t - low
            keys = pl.ds(pl.multiple_of(i * t + low, sub), many)
            here = pl.ds(pl.multiple_of(i * t + low, sub), sub)
            age = lax.broadcasted_iota(jnp.int32, (sub, many), 1)
            allowed = (age > lax.broadcasted_iota(jnp.int32, (sub, many), 0)) & (
                age >= oldest - low
            )
            for h in range(heads):
                at = pl.ds(h * DH, DH)
                s = lax.dot_general(
                    qseg[here, at], kbuf[keys, at], (((1,), (1,)), ((), ())),
                    preferred_element_type=jnp.float32,
                )
                s = jnp.where(allowed, s, -1e30)
                peak, total = (value[low:low + sub] for value in held[h])
                top = jnp.maximum(peak, jnp.max(s, axis=1, keepdims=True))
                p = jnp.exp2((s - top) * SCORE)
                fade = jnp.exp2((peak - top) * SCORE)
                total = total * fade + jnp.sum(p, axis=1, keepdims=True)
                o = acc[pl.ds(low, sub), at] * fade + jnp.dot(
                    p.astype(jnp.bfloat16), vbuf[keys, at], preferred_element_type=jnp.float32
                )
                ho[pl.ds(low, sub), at] = (o / total).astype(jnp.bfloat16)

            spot = pl.ds(low, sub)

            def project(side, c):
                at = pl.ds(pl.multiple_of(side * half + c * chunk, DH), chunk)
                return jnp.dot(ho[spot, :], w_ref[:, at], preferred_element_type=jnp.float32)

            for c in range(NC):
                sib_out[i, spot, pl.ds(c * chunk, chunk)] = project(1 - core, c).astype(
                    jnp.bfloat16
                )
                to_sibling(i, part, c).start()
            for c in range(NC):
                at = pl.ds(c * chunk, chunk)
                mine = project(core, c)
                to_sibling(i, part, c).wait_recv()
                both = mine + sib_in[i, spot, at].astype(jnp.float32)
                comb[i, spot, at] = both.astype(jnp.bfloat16)

                @pl.when(me == i)
                def _():
                    keep(i, part, c).start()

                @pl.when(me != i)
                def _():
                    to_owner(i, part, c, me, i).start()

        return carry

    lax.fori_loop(0, nh, block, 0)

    pieces = [(part, c) for part in reversed(range(NS)) for c in range(NC)]
    for part, c in pieces:
        keep(me, part, c).wait()
        for jx, jc in arrival:
            source = partner(jx, jc)
            to_owner(source, part, c, source, source).wait_recv()

    for jx, jc in arrival:
        peer = partner(jx, jc)
        swap(1, v_hbm, vbuf, 2 * seg, peer, me).wait_send()
        swap(0, kn, kbuf, 2 * seg, peer, me).wait_send()
        swap(2, qn, qseg, 0, peer, me).wait_send()
        for part, c in pieces:
            to_owner(peer, part, c, me, peer).wait_send()

    def sent(i, carry):
        for kind, buf in ((0, kbuf), (1, vbuf)):
            hop(piece(buf, 2 * seg, i), buf, kind, seg, i, h1_s, h1_r).wait_send()
            for part in range(NS):
                pass_on(kind, buf, i, part).wait_send()
        for part, c in pieces:
            to_sibling(i, part, c).wait_send()
        return carry

    lax.fori_loop(0, nh, sent, 0)


def line_kernel(
    q_hbm, k_hbm, v_hbm, scale_ref, w_hbm, start_ref, out_ref,
    rbuf, qin, kin, qn, kn, w_ref, qseg, kbuf, vbuf, gq, xsrc, xin, go, gin, gst, gst_in, low_log,
    low_in, turn, wide_turn, far_log, near_log, acc, own_log, acc_prev, prev_log, ho, sib_out, sib_in, comb,
    load_sem, loc_sem, keep_sem, a2a_s, a2a_r, qa_s, qa_r, kv_s, kv_r, rl_s, gq_s, gq_r, x_s, x_r,
    go_s, go_r, st_s, st_r, sib_s, sib_r, red_s, red_r,
):
    nh, nb = 4, 4
    t, hd = qin.shape
    cols = hd // nh
    heads = cols // DH
    seg = nh * t
    sub = t // 2
    width = w_ref.shape[1]
    half = width // 2
    chunk = half // NC
    nx = nh // 2
    me = lax.axis_index("head")
    z = lax.axis_index("blk")
    chip = me // 2
    core = me % 2
    sib = chip * 2 + (1 - core)

    def partner(jx, jc):
        return ((chip + jx) % nx) * 2 + (core + jc) % 2

    others = [(jx, 0) for jx in range(1, nx)] + [(jx, 1) for jx in range(nx)]
    arrival = [(jx, jc) for jx in range(nx) for jc in range(2) if jx or jc]

    loads = [
        pltpu.make_async_copy(k_hbm, kin, load_sem.at[0]),
        pltpu.make_async_copy(q_hbm, qin, load_sem.at[1]),
        pltpu.make_async_copy(w_hbm, w_ref, load_sem.at[2]),
    ]
    for copy in loads:
        copy.start()

    barrier = pltpu.get_barrier_semaphore()
    for jx, jc in others:
        pl.semaphore_signal(barrier, inc=1, device_id={"head": partner(jx, jc)})
    for d in range(1, nb):
        pl.semaphore_signal(barrier, inc=1, device_id={"blk": (z + d) % nb})
    pl.semaphore_wait(barrier, nh + nb - 2)

    def group(ref, peer):
        return ref.at[:, pl.ds(pl.multiple_of(peer * cols, DH), cols)]

    def piece(ref, base, index):
        return ref.at[pl.ds(pl.multiple_of(base + index * t, t), t), :]

    def swap(kind, src, dst, base, peer, source):
        return pltpu.make_async_remote_copy(
            src_ref=group(src, peer), dst_ref=piece(dst, base, source),
            send_sem=a2a_s.at[kind, peer], recv_sem=a2a_r.at[kind, source],
            device_id={"head": peer},
        )

    def spot(i, part):
        return ((i % 2) * 2 + part) * t + (i // 2) * sub

    def swap_q(part, peer, source):
        return pltpu.make_async_remote_copy(
            src_ref=qn.at[pl.ds(part * sub, sub), pl.ds(pl.multiple_of(peer * cols, DH), cols)],
            dst_ref=qseg.at[pl.ds(pl.multiple_of(spot(source, part), sub), sub), :],
            send_sem=qa_s.at[part, peer], recv_sem=qa_r.at[part, source],
            device_id={"head": peer},
        )

    def own_half(part):
        return pltpu.make_async_copy(
            qn.at[pl.ds(part * sub, sub), pl.ds(pl.multiple_of(me * cols, DH), cols)],
            qseg.at[pl.ds(pl.multiple_of(spot(me, part), sub), sub), :], loc_sem.at[2 + part],
        )

    far = jnp.where(z == 3, 1, 0)
    hop_base = jnp.where(z == 3, 0, seg)
    hop_to = jnp.where(z == 3, 1, z + 1)

    def hop(src, dst, kind, index):
        return pltpu.make_async_remote_copy(
            src_ref=src, dst_ref=piece(dst, hop_base, index),
            send_sem=kv_s.at[kind, index], recv_sem=kv_r.at[far, kind, index],
            device_id={"blk": hop_to},
        )

    def landed(dst, slot, kind, index):
        return pltpu.make_async_remote_copy(
            src_ref=piece(dst, (1 - slot) * seg, index), dst_ref=piece(dst, (1 - slot) * seg, index),
            send_sem=kv_s.at[kind, index], recv_sem=kv_r.at[slot, kind, index],
            device_id={"blk": hop_to},
        )

    def relay(dst, kind, index):
        return pltpu.make_async_remote_copy(
            src_ref=piece(dst, 0, index), dst_ref=piece(dst, seg, index),
            send_sem=rl_s.at[kind, index], recv_sem=kv_r.at[0, kind, index],
            device_id={"blk": 0},
        )

    def normed(src, dst, peer, factor):
        for h in range(heads):
            at = pl.ds(pl.multiple_of(peer * cols + h * DH, DH), DH)
            x = src[:, at].astype(jnp.float32)
            x = x * lax.rsqrt(jnp.mean(x * x, axis=1, keepdims=True) + 1e-06)
            dst[:, at] = (x * (scale_ref[:, at] * factor)).astype(jnp.bfloat16)

    bufs = (kbuf, vbuf)

    def pass_back(kind, index):
        @pl.when(z == 1)
        def _():
            landed(bufs[kind], 1, kind, index).wait_recv()
            relay(bufs[kind], kind, index).start()

    hop(group(v_hbm, me), vbuf, 1, me).start()
    for jx, jc in others:
        swap(1, v_hbm, vbuf, 2 * seg, partner(jx, jc), me).start()
    own_v = pltpu.make_async_copy(group(v_hbm, me), piece(vbuf, 2 * seg, me), loc_sem.at[1])
    own_v.start()

    loads[0].wait()
    normed(kin, kn, me, 1.0)
    hop(group(kn, me), kbuf, 0, me).start()
    own_k = pltpu.make_async_copy(group(kn, me), piece(kbuf, 2 * seg, me), loc_sem.at[0])
    own_k.start()
    for jx, jc in others:
        peer = partner(jx, jc)
        normed(kin, kn, peer, 1.0)
        swap(0, kn, kbuf, 2 * seg, peer, me).start()
    loads[1].wait()
    for jx, jc in others + [(0, 0)]:
        peer = partner(jx, jc)
        normed(qin, qn, peer, SCORE)
        if jx or jc:
            for part in range(2):
                swap_q(part, peer, me).start()
    own_q = [own_half(0), own_half(1)]
    for copy in own_q:
        copy.start()

    def onward(kind, src, buf, jx, jc):
        source = partner(jx, jc)
        swap(kind, src, buf, 2 * seg, source, source).wait_recv()
        hop(piece(buf, 2 * seg, source), buf, kind, source).start()

    onward(1, v_hbm, vbuf, 0, 1)
    onward(0, kn, kbuf, 0, 1)
    pass_back(1, me)
    pass_back(0, me)
    for jx, jc in arrival[1:]:
        onward(1, v_hbm, vbuf, jx, jc)
    pass_back(1, sib)
    pass_back(0, sib)
    first = start_ref[0] - me * t
    both = 2 * t

    def ask(p):
        return pltpu.make_async_remote_copy(
            src_ref=piece(qseg, 0, p), dst_ref=piece(gq, 0, p),
            send_sem=gq_s.at[p], recv_sem=gq_r.at[p], device_id={"blk": z - 1},
        )

    def ask_low(p):
        return pltpu.make_async_remote_copy(
            src_ref=qseg.at[pl.ds(pl.multiple_of(p * t, t), sub), :],
            dst_ref=gq.at[pl.ds(pl.multiple_of(p * sub, sub), sub), :],
            send_sem=gq_s.at[p], recv_sem=gq_r.at[p], device_id={"blk": z - 1},
        )

    def cross(n):
        return pltpu.make_async_remote_copy(
            src_ref=piece(xsrc, 0, n), dst_ref=piece(xin, 0, n),
            send_sem=x_s.at[n], recv_sem=x_r.at[n], device_id={"blk": 2},
        )

    for jx, jc in arrival[1:]:
        source = partner(jx, jc)
        swap(0, kn, kbuf, 2 * seg, source, source).wait_recv()

        @pl.when(z != 0)
        def _():
            hop(piece(kbuf, 2 * seg, source), kbuf, 0, source).start()

    for jx, jc in arrival:
        source = partner(jx, jc)
        for part in range(2):
            swap_q(part, source, source).wait_recv()
    for copy in own_q:
        copy.wait()
    own_v.wait()
    own_k.wait()

    def choose(pair):
        later = first >= 2 * seg
        for part, buf in ((0, kbuf), (1, vbuf)):
            n = 2 * pair + part
            for h in range(heads):
                at = pl.ds(h * DH, DH)
                xsrc[pl.ds(n * t, t), at] = jnp.where(
                    later, qseg[pl.ds(n * t, t), at],
                    buf[pl.ds(2 * seg + (3 - pair) * t, t), at],
                )
            cross(n).start()

    @pl.when(z == 0)
    def _():
        choose(0)
        for jx, jc in arrival[1:]:
            source = partner(jx, jc)
            hop(piece(kbuf, 2 * seg, source), kbuf, 0, source).start()
        choose(1)

    for jx, jc in arrival[1:]:
        pass_back(1, partner(jx, jc))

    @pl.when(z == 3)
    def _():
        def send(step, carry):
            ask(nh - 1 - step).start()
            return carry

        lax.fori_loop(0, nh, send, 0)

    @pl.when(z == 2)
    def _():
        def send(step, carry):
            ask_low(nh - 1 - step).start()
            return carry

        lax.fori_loop(0, nh, send, 0)

    def weigh(q, keys, values, allowed):
        s = lax.dot_general(
            q, keys, (((1,), (1,)), ((), ())), preferred_element_type=jnp.float32
        )
        if allowed is not None:
            s = jnp.where(allowed, s, -1e30)
        peak = jnp.max(s, axis=1, keepdims=True)
        p = jnp.exp2(s - peak).astype(jnp.bfloat16)
        wide = jnp.concatenate([values, jnp.ones(values.shape, jnp.bfloat16)], axis=1)
        out = jnp.dot(p, wide, preferred_element_type=jnp.float32)
        return peak, out[:, DH:], out[:, :DH]

    def partial(size, q_of, k_of, v_of, allowed, put):
        lane = lax.broadcasted_iota(jnp.int32, (size, DH), 1)
        logs = jnp.zeros((size, DH), jnp.float32)
        for h in range(heads):
            at = pl.ds(h * DH, DH)
            peak, total, o = weigh(q_of(at), k_of(at), v_of(at), allowed)
            put(at, o / total)
            logs = jnp.where(lane == h, peak + jnp.log(total) * LOG2E, logs)
        return logs

    def cut(ref, base, size):
        rows = pl.ds(pl.multiple_of(base, sub), size)
        return lambda at: ref[rows, at]

    def into(ref, base, size):
        rows = pl.ds(pl.multiple_of(base, sub), size)

        def put(at, value):
            ref[rows, at] = value.astype(ref.dtype)

        return put

    def pair_rows(pair):
        return pl.ds(pl.multiple_of(pair * both, both), both)

    def ages(pair):
        r = lax.broadcasted_iota(jnp.int32, (both, seg), 0)
        upper = jnp.where(r < t + sub, r - sub, r + both - t)
        return jnp.where(r < sub, r, jnp.where(r < t, r + both - sub, upper)) + pair * t

    col = lax.broadcasted_iota(jnp.int32, (both, seg), 1)

    def own_part(pair, carry):
        own_log[pair_rows(pair), :] = partial(
            both, cut(qseg, pair * both, both), cut(kbuf, 2 * seg, seg), cut(vbuf, 2 * seg, seg),
            col <= ages(pair), into(acc, pair * both, both),
        )
        return carry

    lax.fori_loop(0, 2, own_part, 0)

    for jx, jc in arrival[1:]:
        pass_back(0, partner(jx, jc))
    loads[2].wait()

    def stats(e, p, to):
        return pltpu.make_async_remote_copy(
            src_ref=gst.at[e, p], dst_ref=gst_in.at[p],
            send_sem=st_s.at[e, p], recv_sem=st_r.at[p], device_id={"blk": to},
        )

    def answer(e, p, to):
        return [
            pltpu.make_async_remote_copy(
                src_ref=piece(go.at[e], 0, p), dst_ref=piece(gin, 0, p),
                send_sem=go_s.at[e, p], recv_sem=go_r.at[p], device_id={"blk": to},
            ),
            stats(e, p, to),
        ]

    def low_answer(p):
        return pltpu.make_async_remote_copy(
            src_ref=go.at[0, pl.ds(pl.multiple_of(p * sub, sub), sub), :],
            dst_ref=gin.at[pl.ds(pl.multiple_of(p * t, t), sub), :],
            send_sem=go_s.at[0, p], recv_sem=go_r.at[p], device_id={"blk": 2},
        )

    low_stats = pltpu.make_async_remote_copy(
        src_ref=low_log, dst_ref=low_in,
        send_sem=st_s.at[0, 0], recv_sem=st_r.at[0], device_id={"blk": 2},
    )

    def serve(e, pair, q_ref, base, to):
        logs = partial(
            both, cut(q_ref, pair * both, both), cut(kbuf, base, seg), cut(vbuf, base, seg),
            col > ages(pair), into(go.at[e], pair * both, both),
        ).T[:heads]
        for n in range(2):
            gst[e, 2 * pair + n] = logs[:, n * t:(n + 1) * t]
        for n in (1, 0):
            for copy in answer(e, 2 * pair + n, to):
                copy.start()

    def help_across(pair):
        for n in range(2):
            cross(2 * pair + n).wait_recv()
        serve(1, pair, xin, 2 * seg, 0)

    def help_next(pair):
        for n in range(2):
            ask(2 * pair + n).wait_recv()
        serve(0, pair, gq, seg, 3)

    @pl.when(z == 2)
    def _():
        help_across(0)

    def prev_in(i, carry):
        for kind in range(2):
            landed(bufs[kind], 0, kind, i).wait_recv()
        return carry

    lax.fori_loop(0, nh, prev_in, 0)

    turn[...] = jnp.zeros_like(turn)
    wide_turn[...] = jnp.zeros_like(wide_turn)

    @pl.when(z == 1)
    def _():
        for p in range(nh):
            ask_low(p).wait_recv()
        low_log[...] = partial(
            both, cut(gq, 0, both), cut(kbuf, seg, seg), cut(vbuf, seg, seg),
            col > lax.broadcasted_iota(jnp.int32, (both, seg), 0), into(go.at[0], 0, both),
        ).T[:heads]
        low_stats.start()
        for p in reversed(range(nh)):
            low_answer(p).start()

    def to_sibling(i, c):
        at = (i, slice(None), pl.ds(c * chunk, chunk))
        return pltpu.make_async_remote_copy(
            src_ref=sib_out.at[at], dst_ref=sib_in.at[at],
            send_sem=sib_s.at[i, c], recv_sem=sib_r.at[i, c],
            device_id={"head": sib},
        )

    def home(x, side, part, c):
        columns = pl.ds(pl.multiple_of(side * half + c * chunk, DH), chunk)
        return rbuf.at[x, pl.ds(pl.multiple_of(part * sub, sub), sub), columns]

    def strip(p, x, c):
        return comb.at[p, pl.ds(x * sub, sub), pl.ds(c * chunk, chunk)]

    def to_owner(p, x, c, source, owner):
        return pltpu.make_async_remote_copy(
            src_ref=strip(p, x, c), dst_ref=home(source // 2, source % 2, p % 2, c),
            send_sem=red_s.at[p, x, c], recv_sem=red_r.at[source, p % 2, c],
            device_id={"head": owner},
        )

    def keep(p, x, c):
        return pltpu.make_async_copy(
            strip(p, x, c), home(chip, core, p % 2, c), keep_sem.at[p % 2, c],
        )

    def near_part(pair, count):
        rows = [pl.ds((2 * pair + n) * t + sub, sub) for n in range(2)]

        def newest(first_slot):
            def of(at):
                last = xin[pl.ds(first_slot * t, t), at]
                if count == t:
                    return last
                return jnp.concatenate([xin[pl.ds((first_slot + 2) * t, t), at], last], axis=0)

            return of

        def put(at, value):
            for n in range(2):
                gin[rows[n], at] = value[n * sub:(n + 1) * sub].astype(gin.dtype)

        far_log[pl.ds(pair * t, t), :] = partial(
            t, lambda at: jnp.concatenate([qseg[rows[0], at], qseg[rows[1], at]], axis=0),
            newest(0), newest(1),
            lax.broadcasted_iota(jnp.int32, (t, count), 1)
            > lax.broadcasted_iota(jnp.int32, (t, count), 0), put,
        )

    def prev_part(pair):
        prev_log[pair_rows(pair), :] = partial(
            both, cut(qseg, pair * both, both), cut(kbuf, seg, seg), cut(vbuf, seg, seg), None,
            into(acc_prev, pair * both, both),
        )

    def turn_pair(step):
        pair = jnp.where(z == 0, step, 1 - step)

        @pl.when((z != 2) | (step == 0))
        def _():
            prev_part(pair)

        @pl.when(z == 1)
        def _():
            far_log[pair_rows(pair), :] = partial(
                both, cut(qseg, pair * both, both), cut(kbuf, 0, seg), cut(vbuf, 0, seg),
                col > ages(pair), into(gin, pair * both, both),
            )

        @pl.when((z == 2) & (step == 0))
        def _():
            help_next(1)
            near_part(1, t)
            help_next(0)
            prev_part(0)
            help_across(1)

        @pl.when((z == 2) & (step == 1))
        def _():
            near_part(0, both)

    def block(step, carry):
        @pl.when(step % 2 == 0)
        def _():
            turn_pair(step // 2)

        i = jnp.where(z == 0, step // 2 * 2 + 1 - step % 2, nh - 1 - step)
        rows = pl.ds(pl.multiple_of(i * t, t), t)

        @pl.when(z == 1)
        def _():
            near_log[...] = far_log[rows, :]

        @pl.when((z == 2) & (step == 0))
        def _():
            low_stats.wait_recv()
            wide_turn[:heads] = low_in[...]
            far_log[both:] = wide_turn[...].T

        @pl.when(z == 2)
        def _():
            low_answer(i).wait_recv()
            near_log[:sub] = far_log[pl.ds(pl.multiple_of(both + i * sub, sub), sub), :]
            near_log[sub:] = far_log[pl.ds(pl.multiple_of(i * sub, sub), sub), :]

        @pl.when((z == 0) | (z == 3))
        def _():
            for copy in answer(0, i, 0):
                copy.wait_recv()
            turn[:heads] = gst_in[i]
            near_log[...] = turn[...].T

        own = own_log[rows, :]
        before = jnp.where(first >= seg, prev_log[rows, :], -1e30)
        logs = jnp.where(first >= 2 * seg, near_log[...], -1e30)
        top = jnp.maximum(jnp.maximum(own, before), logs)
        own, before, logs = jnp.exp2(own - top), jnp.exp2(before - top), jnp.exp2(logs - top)
        share = 1.0 / (own + before + logs)
        own, before, logs = own * share, before * share, logs * share
        for h in range(heads):
            at = pl.ds(h * DH, DH)
            o = acc[rows, at] * own[:, h:h + 1] + acc_prev[rows, at] * before[:, h:h + 1]
            o = o + gin[rows, at].astype(jnp.float32) * logs[:, h:h + 1]
            ho[:, at] = o.astype(jnp.bfloat16)

        def project(side, c):
            at = pl.ds(pl.multiple_of(side * half + c * chunk, DH), chunk)
            return jnp.dot(ho[...], w_ref[:, at], preferred_element_type=jnp.float32)

        for c in range(NC):
            sib_out[i, :, pl.ds(c * chunk, chunk)] = project(1 - core, c).astype(jnp.bfloat16)
            to_sibling(i, c).start()
        for c in range(NC):
            at = pl.ds(c * chunk, chunk)
            mine = project(core, c)
            to_sibling(i, c).wait_recv()
            whole = mine + sib_in[i, :, at].astype(jnp.float32)
            comb[i, :, at] = whole.astype(jnp.bfloat16)
            for x in range(2):
                owner = i // 2 + 2 * x

                @pl.when(me == owner)
                def _():
                    keep(i, x, c).start()

                @pl.when(me != owner)
                def _():
                    to_owner(i, x, c, me, owner).start()

        return carry

    lax.fori_loop(0, nh, block, 0)

    for step in range(2):
        part = jnp.where(z == 0, step, 1 - step)
        for c in range(NC):
            keep((me % 2) * 2 + part, 0, c).wait()
            for jx, jc in arrival:
                source = partner(jx, jc)
                to_owner(part, 0, c, source, source).wait_recv()
            rows = pl.ds(pl.multiple_of(part * sub, sub), sub)
            for side in range(2):
                at = pl.ds(side * half + c * chunk, chunk)
                out_ref[rows, at] = (
                    rbuf[0, rows, at].astype(jnp.float32) + rbuf[1, rows, at].astype(jnp.float32)
                ).astype(out_ref.dtype)

    for jx, jc in arrival:
        peer = partner(jx, jc)
        swap(1, v_hbm, vbuf, 2 * seg, peer, me).wait_send()
        swap(0, kn, kbuf, 2 * seg, peer, me).wait_send()
        for part in range(2):
            swap_q(part, peer, me).wait_send()

    def sent(i, carry):
        for c in range(NC):
            to_sibling(i, c).wait_send()
            for x in range(2):
                owner = i // 2 + 2 * x

                @pl.when(me != owner)
                def _():
                    to_owner(i, x, c, me, owner).wait_send()

        @pl.when(z == 1)
        def _():
            for kind in range(2):
                relay(bufs[kind], kind, i).wait_send()

        return carry

    lax.fori_loop(0, nh, sent, 0)

    def hop_sent(i, carry):
        for kind in range(2):
            hop(piece(bufs[kind], 2 * seg, i), bufs[kind], kind, i).wait_send()
        return carry

    lax.fori_loop(0, nh, hop_sent, 0)

    @pl.when(z == 0)
    def _():
        for n in range(nh):
            cross(n).wait_send()

    @pl.when(z == 1)
    def _():
        low_stats.wait_send()
        for p in range(nh):
            low_answer(p).wait_send()

    @pl.when(z == 2)
    def _():
        for p in range(nh):
            ask_low(p).wait_send()
        for i in range(nh):
            for copy in answer(0, i, 3) + answer(1, i, 0):
                copy.wait_send()

    @pl.when(z == 3)
    def _():
        for i in range(nh):
            ask(i).wait_send()


def line_call(queries, keys, values, scale, w_out, stretch_start):
    nh = 4
    t, hd = queries.shape
    cols = hd // nh
    seg = nh * t
    width = w_out.shape[1]
    half = width // 2
    heads = cols // DH
    bf16 = jnp.bfloat16
    f32 = jnp.float32
    dma = pltpu.SemaphoreType.DMA
    anywhere = pl.BlockSpec(memory_space=pltpu.HBM)
    vmem = pl.BlockSpec(memory_space=pltpu.VMEM)
    return pl.pallas_call(
        line_kernel,
        out_shape=pltpu.VMEM((t, width), bf16),
        in_specs=[anywhere, anywhere, anywhere, vmem, anywhere,
                  pl.BlockSpec(memory_space=pltpu.SMEM)],
        out_specs=vmem,
        scratch_shapes=[
            pltpu.VMEM((nh // 2, t, width), bf16),
            pltpu.VMEM((t, hd), bf16),
            pltpu.VMEM((t, hd), bf16),
            pltpu.VMEM((t, hd), bf16),
            pltpu.VMEM((t, hd), bf16),
            pltpu.VMEM((cols, width), bf16),
            pltpu.VMEM((seg, cols), bf16),
            pltpu.VMEM((3 * seg, cols), bf16),
            pltpu.VMEM((3 * seg, cols), bf16),
            pltpu.VMEM((seg, cols), bf16),
            pltpu.VMEM((seg, cols), bf16),
            pltpu.VMEM((seg, cols), bf16),
            pltpu.VMEM((2, seg, cols), bf16),
            pltpu.VMEM((seg, cols), bf16),
            pltpu.VMEM((2, nh, heads, t), f32),
            pltpu.VMEM((nh, heads, t), f32),
            pltpu.VMEM((heads, 2 * t), f32),
            pltpu.VMEM((heads, 2 * t), f32),
            pltpu.VMEM((DH, t), f32),
            pltpu.VMEM((DH, 2 * t), f32),
            pltpu.VMEM((seg, DH), f32),
            pltpu.VMEM((t, DH), f32),
            pltpu.VMEM((seg, cols), f32),
            pltpu.VMEM((seg, DH), f32),
            pltpu.VMEM((seg, cols), f32),
            pltpu.VMEM((seg, DH), f32),
            pltpu.VMEM((t, cols), bf16),
            pltpu.VMEM((nh, t, half), bf16),
            pltpu.VMEM((nh, t, half), bf16),
            pltpu.VMEM((nh, t, half), bf16),
            dma((3,)),
            dma((4,)),
            dma((2, NC)),
            dma((2, nh)),
            dma((2, nh)),
            dma((2, nh)),
            dma((2, nh)),
            dma((2, nh)),
            dma((2, 2, nh)),
            dma((2, nh)),
            dma((nh,)),
            dma((nh,)),
            dma((nh,)),
            dma((nh,)),
            dma((2, nh)),
            dma((nh,)),
            dma((2, nh)),
            dma((nh,)),
            dma((nh, NC)),
            dma((nh, NC)),
            dma((nh, 2, NC)),
            dma((nh, 2, NC)),
        ],
        compiler_params=pltpu.CompilerParams(
            collective_id=0, has_side_effects=True,
            vmem_limit_bytes=54 * 1024 * 1024,
        ),
    )(queries, keys, values, scale, w_out, stretch_start)


def solution(mesh):
    nh = mesh.shape["head"]
    nb = mesh.shape["blk"]

    def shards(queries, keys, values, scale_qk, w_out, stretch_start):
        if nb == 4 and nh == 4:
            return line_call(
                queries, keys, values, scale_qk.reshape(1, -1), w_out, stretch_start
            )
        t, hd = queries.shape
        cols = hd // nh
        seg = nh * t
        width = w_out.shape[1]
        half = width // 2
        bf16 = jnp.bfloat16
        dma = pltpu.SemaphoreType.DMA
        anywhere = pl.BlockSpec(memory_space=pltpu.HBM)
        vmem = pl.BlockSpec(memory_space=pltpu.VMEM)
        parts = pl.pallas_call(
            functools.partial(kernel, nh, nb),
            out_shape=pltpu.VMEM((nh // 2, t, width), bf16),
            in_specs=[anywhere, anywhere, anywhere, vmem, anywhere,
                      pl.BlockSpec(memory_space=pltpu.SMEM)],
            out_specs=vmem,
            scratch_shapes=[
                pltpu.VMEM((t, hd), bf16),
                pltpu.VMEM((t, hd), bf16),
                pltpu.VMEM((t, hd), bf16),
                pltpu.VMEM((t, hd), bf16),
                pltpu.VMEM((cols, width), bf16),
                pltpu.VMEM((seg, cols), bf16),
                pltpu.VMEM((3 * seg, cols), bf16),
                pltpu.VMEM((3 * seg, cols), bf16),
                pltpu.VMEM((t, cols), jnp.float32),
                pltpu.VMEM((t, cols), bf16),
                pltpu.VMEM((nh, t, half), bf16),
                pltpu.VMEM((nh, t, half), bf16),
                pltpu.VMEM((nh, t, half), bf16),
                dma((3,)),
                dma((3,)),
                dma((NS, NC)),
                dma((3, nh)),
                dma((3, nh)),
                dma((2, nh)),
                dma((2, nh)),
                dma((2, nh, NS)),
                dma((2, nh, NS)),
                dma((nh, NS, NC)),
                dma((nh, NS, NC)),
                dma((nh, NS, NC)),
                dma((nh, NS, NC)),
            ],
            compiler_params=pltpu.CompilerParams(
                collective_id=0, has_side_effects=True, vmem_limit_bytes=54 * 1024 * 1024
            ),
        )(queries, keys, values, scale_qk.reshape(1, hd), w_out, stretch_start)
        return jnp.sum(parts.astype(jnp.float32), axis=0).astype(bf16)

    return jax.shard_map(
        shards,
        mesh=mesh,
        in_specs=(
            P(("groups", "blk", "head"), None),
            P(("groups", "blk", "head"), None),
            P(("groups", "blk", "head"), None),
            P(),
            P("head", None),
            P(("groups", "blk", "head")),
        ),
        out_specs=P(("groups", "blk", "head"), None),
        check_vma=False,
    )
```

```python
import functools

import jax
import jax.numpy as jnp
from jax import lax
from jax.experimental import pallas as pl
from jax.experimental.pallas import tpu as pltpu
from jax.sharding import PartitionSpec as P

DH = 128
LOG2E = 1.4426950408889634
SCORE = LOG2E / DH**0.5
NC = 4
NS = 2


def kernel(
    nh, nb, q_hbm, k_hbm, v_hbm, scale_ref, w_hbm, start_ref, rbuf,
    qin, kin, qn, kn, w_ref, qseg, kbuf, vbuf, acc, ho, sib_out, sib_in, comb,
    load_sem, loc_sem, keep_sem, a2a_s, a2a_r, h1_s, h1_r, h2_s, h2_r, sib_s, sib_r, red_s, red_r,
):
    t, hd = qin.shape
    cols = hd // nh
    heads = cols // DH
    seg = nh * t
    sub = t // NS
    width = w_ref.shape[1]
    half = width // 2
    chunk = half // NC
    nx = nh // 2
    me = lax.axis_index("head")
    z = lax.axis_index("blk")
    chip = me // 2
    core = me % 2
    sib = chip * 2 + (1 - core)
    nxt = (z + 1) % nb
    prv = (z + nb - 1) % nb

    def partner(jx, jc):
        return ((chip + jx) % nx) * 2 + (core + jc) % 2

    others = [(jx, 0) for jx in range(1, nx)] + [(jx, 1) for jx in range(nx)]
    arrival = [(jx, jc) for jx in range(nx) for jc in range(2) if jx or jc]

    loads = [
        pltpu.make_async_copy(k_hbm, kin, load_sem.at[0]),
        pltpu.make_async_copy(q_hbm, qin, load_sem.at[1]),
        pltpu.make_async_copy(w_hbm, w_ref, load_sem.at[2]),
    ]
    for copy in loads:
        copy.start()

    barrier = pltpu.get_barrier_semaphore()
    for jx, jc in others:
        pl.semaphore_signal(barrier, inc=1, device_id={"head": partner(jx, jc)})
    pl.semaphore_signal(barrier, inc=1, device_id={"blk": nxt})
    pl.semaphore_signal(barrier, inc=1, device_id={"blk": prv})
    pl.semaphore_wait(barrier, nh + 1)

    def group(ref, peer):
        return ref.at[:, pl.ds(pl.multiple_of(peer * cols, DH), cols)]

    def piece(ref, base, index):
        return ref.at[pl.ds(pl.multiple_of(base + index * t, t), t), :]

    def swap(kind, src, dst, base, peer, source):
        return pltpu.make_async_remote_copy(
            src_ref=group(src, peer), dst_ref=piece(dst, base, source),
            send_sem=a2a_s.at[kind, peer], recv_sem=a2a_r.at[kind, source],
            device_id={"head": peer},
        )

    def hop(src, dst, kind, base, index, send, recv):
        return pltpu.make_async_remote_copy(
            src_ref=src, dst_ref=piece(dst, base, index),
            send_sem=send.at[kind, index], recv_sem=recv.at[kind, index],
            device_id={"blk": nxt},
        )

    def normed(src, dst, peer):
        for h in range(heads):
            at = pl.ds(pl.multiple_of(peer * cols + h * DH, DH), DH)
            x = src[:, at].astype(jnp.float32)
            x = x * lax.rsqrt(jnp.mean(x * x, axis=1, keepdims=True) + 1e-06)
            dst[:, at] = (x * scale_ref[:, at]).astype(jnp.bfloat16)

    hop(group(v_hbm, me), vbuf, 1, seg, me, h1_s, h1_r).start()
    for jx, jc in others:
        swap(1, v_hbm, vbuf, 2 * seg, partner(jx, jc), me).start()
    own_v = pltpu.make_async_copy(group(v_hbm, me), piece(vbuf, 2 * seg, me), loc_sem.at[1])
    own_v.start()

    loads[0].wait()
    normed(kin, kn, me)
    hop(group(kn, me), kbuf, 0, seg, me, h1_s, h1_r).start()
    own_k = pltpu.make_async_copy(group(kn, me), piece(kbuf, 2 * seg, me), loc_sem.at[0])
    own_k.start()
    for jx, jc in others:
        peer = partner(jx, jc)
        normed(kin, kn, peer)
        swap(0, kn, kbuf, 2 * seg, peer, me).start()

    loads[1].wait()
    for jx, jc in [(0, 0)] + others:
        normed(qin, qn, partner(jx, jc))
    own_q = pltpu.make_async_copy(group(qn, me), piece(qseg, 0, me), loc_sem.at[2])
    own_q.start()

    def onward(kind, src, buf, jx, jc):
        source = partner(jx, jc)
        swap(kind, src, buf, 2 * seg, source, source).wait_recv()
        hop(piece(buf, 2 * seg, source), buf, kind, seg, source, h1_s, h1_r).start()

    onward(1, v_hbm, vbuf, 0, 1)
    onward(0, kn, kbuf, 0, 1)
    for jx, jc in arrival[1:]:
        onward(1, v_hbm, vbuf, jx, jc)
    for jx, jc in arrival[1:]:
        onward(0, kn, kbuf, jx, jc)
    for jx, jc in others:
        peer = partner(jx, jc)
        swap(2, qn, qseg, 0, peer, me).start()

    def slab(ref, base, i, part):
        return ref.at[pl.ds(pl.multiple_of(base + i * t + part * sub, sub), sub), :]

    def pass_on(kind, buf, i, part):
        return pltpu.make_async_remote_copy(
            src_ref=slab(buf, seg, i, part), dst_ref=slab(buf, 0, i, part),
            send_sem=h2_s.at[kind, i, part], recv_sem=h2_r.at[kind, i, part],
            device_id={"blk": nxt},
        )

    def relay(step, carry):
        i = nh - 1 - step
        for kind, buf in ((0, kbuf), (1, vbuf)):
            hop(piece(buf, 2 * seg, i), buf, kind, seg, i, h1_s, h1_r).wait_recv()
        for part in reversed(range(NS)):
            for kind, buf in ((0, kbuf), (1, vbuf)):
                pass_on(kind, buf, i, part).start()
        return carry

    lax.fori_loop(0, nh, relay, 0)
    for jx, jc in arrival:
        source = partner(jx, jc)
        swap(2, qn, qseg, 0, source, source).wait_recv()
    own_q.wait()
    own_k.wait()
    own_v.wait()
    loads[2].wait()

    first = start_ref[0] - me * t
    row = lax.broadcasted_iota(jnp.int32, (t, 2 * seg), 0)
    col = lax.broadcasted_iota(jnp.int32, (t, 2 * seg), 1)

    def to_sibling(i, part, c):
        at = (i, pl.ds(part * sub, sub), pl.ds(c * chunk, chunk))
        return pltpu.make_async_remote_copy(
            src_ref=sib_out.at[at], dst_ref=sib_in.at[at],
            send_sem=sib_s.at[i, part, c], recv_sem=sib_r.at[i, part, c],
            device_id={"head": sib},
        )

    def home(x, side, part, c):
        columns = pl.ds(pl.multiple_of(side * half + c * chunk, DH), chunk)
        return rbuf.at[x, pl.ds(part * sub, sub), columns]

    def to_owner(i, part, c, source, owner):
        return pltpu.make_async_remote_copy(
            src_ref=comb.at[i, pl.ds(part * sub, sub), pl.ds(c * chunk, chunk)],
            dst_ref=home(source // 2, source % 2, part, c),
            send_sem=red_s.at[i, part, c], recv_sem=red_r.at[source, part, c],
            device_id={"head": owner},
        )

    def keep(i, part, c):
        return pltpu.make_async_copy(
            comb.at[i, pl.ds(part * sub, sub), pl.ds(c * chunk, chunk)],
            home(chip, core, part, c), keep_sem.at[part, c],
        )

    def block(step, carry):
        i = nh - 1 - step
        rows = pl.ds(pl.multiple_of(i * t, t), t)
        keys = pl.ds(pl.multiple_of(i * t + t, t), 2 * seg)
        oldest = 2 * seg - first - i * t
        allowed = (col <= row + (2 * seg - t)) & (col >= oldest - t)
        held = []
        for h in range(heads):
            at = pl.ds(h * DH, DH)
            s = lax.dot_general(
                qseg[rows, at], kbuf[keys, at], (((1,), (1,)), ((), ())),
                preferred_element_type=jnp.float32,
            )
            s = jnp.where(allowed, s, -1e30)
            peak = jnp.max(s, axis=1, keepdims=True)
            p = jnp.exp2((s - peak) * SCORE)
            held.append((peak, jnp.sum(p, axis=1, keepdims=True)))
            acc[:, at] = jnp.dot(
                p.astype(jnp.bfloat16), vbuf[keys, at], preferred_element_type=jnp.float32
            )

        for part in reversed(range(NS)):
            for kind, buf in ((0, kbuf), (1, vbuf)):
                pass_on(kind, buf, i, part).wait_recv()
            low = part * sub
            many = t - low
            keys = pl.ds(pl.multiple_of(i * t + low, sub), many)
            here = pl.ds(pl.multiple_of(i * t + low, sub), sub)
            age = lax.broadcasted_iota(jnp.int32, (sub, many), 1)
            allowed = (age > lax.broadcasted_iota(jnp.int32, (sub, many), 0)) & (
                age >= oldest - low
            )
            for h in range(heads):
                at = pl.ds(h * DH, DH)
                s = lax.dot_general(
                    qseg[here, at], kbuf[keys, at], (((1,), (1,)), ((), ())),
                    preferred_element_type=jnp.float32,
                )
                s = jnp.where(allowed, s, -1e30)
                peak, total = (value[low:low + sub] for value in held[h])
                top = jnp.maximum(peak, jnp.max(s, axis=1, keepdims=True))
                p = jnp.exp2((s - top) * SCORE)
                fade = jnp.exp2((peak - top) * SCORE)
                total = total * fade + jnp.sum(p, axis=1, keepdims=True)
                o = acc[pl.ds(low, sub), at] * fade + jnp.dot(
                    p.astype(jnp.bfloat16), vbuf[keys, at], preferred_element_type=jnp.float32
                )
                ho[pl.ds(low, sub), at] = (o / total).astype(jnp.bfloat16)

            spot = pl.ds(low, sub)

            def project(side, c):
                at = pl.ds(pl.multiple_of(side * half + c * chunk, DH), chunk)
                return jnp.dot(ho[spot, :], w_ref[:, at], preferred_element_type=jnp.float32)

            for c in range(NC):
                sib_out[i, spot, pl.ds(c * chunk, chunk)] = project(1 - core, c).astype(
                    jnp.bfloat16
                )
                to_sibling(i, part, c).start()
            for c in range(NC):
                at = pl.ds(c * chunk, chunk)
                mine = project(core, c)
                to_sibling(i, part, c).wait_recv()
                both = mine + sib_in[i, spot, at].astype(jnp.float32)
                comb[i, spot, at] = both.astype(jnp.bfloat16)

                @pl.when(me == i)
                def _():
                    keep(i, part, c).start()

                @pl.when(me != i)
                def _():
                    to_owner(i, part, c, me, i).start()

        return carry

    lax.fori_loop(0, nh, block, 0)

    pieces = [(part, c) for part in reversed(range(NS)) for c in range(NC)]
    for part, c in pieces:
        keep(me, part, c).wait()
        for jx, jc in arrival:
            source = partner(jx, jc)
            to_owner(source, part, c, source, source).wait_recv()

    for jx, jc in arrival:
        peer = partner(jx, jc)
        swap(1, v_hbm, vbuf, 2 * seg, peer, me).wait_send()
        swap(0, kn, kbuf, 2 * seg, peer, me).wait_send()
        swap(2, qn, qseg, 0, peer, me).wait_send()
        for part, c in pieces:
            to_owner(peer, part, c, me, peer).wait_send()

    def sent(i, carry):
        for kind, buf in ((0, kbuf), (1, vbuf)):
            hop(piece(buf, 2 * seg, i), buf, kind, seg, i, h1_s, h1_r).wait_send()
            for part in range(NS):
                pass_on(kind, buf, i, part).wait_send()
        for part, c in pieces:
            to_sibling(i, part, c).wait_send()
        return carry

    lax.fori_loop(0, nh, sent, 0)


def line_kernel(
    q_hbm, k_hbm, v_hbm, scale_ref, w_hbm, start_ref, out_ref,
    rbuf, qin, kin, qn, kn, w_ref, qseg, kbuf, vbuf, gq, xsrc, xin, go, gin, gst, gst_in, low_log,
    low_in, turn, wide_turn, far_log, near_log, acc, own_log, acc_prev, prev_log, ho, sib_out, sib_in, comb,
    load_sem, loc_sem, keep_sem, a2a_s, a2a_r, qa_s, qa_r, kv_s, kv_r, rl_s, gq_s, gq_r, x_s, x_r,
    go_s, go_r, st_s, st_r, sib_s, sib_r, red_s, red_r,
):
    nh, nb = 4, 4
    t, hd = qin.shape
    cols = hd // nh
    heads = cols // DH
    seg = nh * t
    sub = t // 2
    width = w_ref.shape[1]
    half = width // 2
    chunk = half // NC
    nx = nh // 2
    me = lax.axis_index("head")
    z = lax.axis_index("blk")
    chip = me // 2
    core = me % 2
    sib = chip * 2 + (1 - core)

    def partner(jx, jc):
        return ((chip + jx) % nx) * 2 + (core + jc) % 2

    others = [(jx, 0) for jx in range(1, nx)] + [(jx, 1) for jx in range(nx)]
    arrival = [(jx, jc) for jx in range(nx) for jc in range(2) if jx or jc]

    loads = [
        pltpu.make_async_copy(k_hbm, kin, load_sem.at[0]),
        pltpu.make_async_copy(q_hbm, qin, load_sem.at[1]),
        pltpu.make_async_copy(w_hbm, w_ref, load_sem.at[2]),
    ]
    for copy in loads:
        copy.start()

    barrier = pltpu.get_barrier_semaphore()
    for jx, jc in others:
        pl.semaphore_signal(barrier, inc=1, device_id={"head": partner(jx, jc)})
    for d in range(1, nb):
        pl.semaphore_signal(barrier, inc=1, device_id={"blk": (z + d) % nb})
    pl.semaphore_wait(barrier, nh + nb - 2)

    def group(ref, peer):
        return ref.at[:, pl.ds(pl.multiple_of(peer * cols, DH), cols)]

    def piece(ref, base, index):
        return ref.at[pl.ds(pl.multiple_of(base + index * t, t), t), :]

    def swap(kind, src, dst, base, peer, source):
        return pltpu.make_async_remote_copy(
            src_ref=group(src, peer), dst_ref=piece(dst, base, source),
            send_sem=a2a_s.at[kind, peer], recv_sem=a2a_r.at[kind, source],
            device_id={"head": peer},
        )

    def spot(i, part):
        return ((i % 2) * 2 + part) * t + (i // 2) * sub

    def swap_q(part, peer, source):
        return pltpu.make_async_remote_copy(
            src_ref=qn.at[pl.ds(part * sub, sub), pl.ds(pl.multiple_of(peer * cols, DH), cols)],
            dst_ref=qseg.at[pl.ds(pl.multiple_of(spot(source, part), sub), sub), :],
            send_sem=qa_s.at[part, peer], recv_sem=qa_r.at[part, source],
            device_id={"head": peer},
        )

    def own_half(part):
        return pltpu.make_async_copy(
            qn.at[pl.ds(part * sub, sub), pl.ds(pl.multiple_of(me * cols, DH), cols)],
            qseg.at[pl.ds(pl.multiple_of(spot(me, part), sub), sub), :], loc_sem.at[2 + part],
        )

    far = jnp.where(z == 3, 1, 0)
    hop_base = jnp.where(z == 3, 0, seg)
    hop_to = jnp.where(z == 3, 1, z + 1)

    def hop(src, dst, kind, index):
        return pltpu.make_async_remote_copy(
            src_ref=src, dst_ref=piece(dst, hop_base, index),
            send_sem=kv_s.at[kind, index], recv_sem=kv_r.at[far, kind, index],
            device_id={"blk": hop_to},
        )

    def landed(dst, slot, kind, index):
        return pltpu.make_async_remote_copy(
            src_ref=piece(dst, (1 - slot) * seg, index), dst_ref=piece(dst, (1 - slot) * seg, index),
            send_sem=kv_s.at[kind, index], recv_sem=kv_r.at[slot, kind, index],
            device_id={"blk": hop_to},
        )

    def relay(dst, kind, index):
        return pltpu.make_async_remote_copy(
            src_ref=piece(dst, 0, index), dst_ref=piece(dst, seg, index),
            send_sem=rl_s.at[kind, index], recv_sem=kv_r.at[0, kind, index],
            device_id={"blk": 0},
        )

    def normed(src, dst, peer, factor):
        for h in range(heads):
            at = pl.ds(pl.multiple_of(peer * cols + h * DH, DH), DH)
            x = src[:, at].astype(jnp.float32)
            x = x * lax.rsqrt(jnp.mean(x * x, axis=1, keepdims=True) + 1e-06)
            dst[:, at] = (x * (scale_ref[:, at] * factor)).astype(jnp.bfloat16)

    bufs = (kbuf, vbuf)

    def pass_back(kind, index):
        @pl.when(z == 1)
        def _():
            landed(bufs[kind], 1, kind, index).wait_recv()
            relay(bufs[kind], kind, index).start()

    hop(group(v_hbm, me), vbuf, 1, me).start()
    for jx, jc in others:
        swap(1, v_hbm, vbuf, 2 * seg, partner(jx, jc), me).start()
    own_v = pltpu.make_async_copy(group(v_hbm, me), piece(vbuf, 2 * seg, me), loc_sem.at[1])
    own_v.start()

    loads[0].wait()
    normed(kin, kn, me, 1.0)
    hop(group(kn, me), kbuf, 0, me).start()
    own_k = pltpu.make_async_copy(group(kn, me), piece(kbuf, 2 * seg, me), loc_sem.at[0])
    own_k.start()
    for jx, jc in others:
        peer = partner(jx, jc)
        normed(kin, kn, peer, 1.0)
        swap(0, kn, kbuf, 2 * seg, peer, me).start()
    loads[1].wait()
    for jx, jc in others + [(0, 0)]:
        peer = partner(jx, jc)
        normed(qin, qn, peer, SCORE)
        if jx or jc:
            for part in range(2):
                swap_q(part, peer, me).start()
    own_q = [own_half(0), own_half(1)]
    for copy in own_q:
        copy.start()

    def onward(kind, src, buf, jx, jc):
        source = partner(jx, jc)
        swap(kind, src, buf, 2 * seg, source, source).wait_recv()
        hop(piece(buf, 2 * seg, source), buf, kind, source).start()

    onward(1, v_hbm, vbuf, 0, 1)
    onward(0, kn, kbuf, 0, 1)
    pass_back(1, me)
    pass_back(0, me)
    for jx, jc in arrival[1:]:
        onward(1, v_hbm, vbuf, jx, jc)
    pass_back(1, sib)
    pass_back(0, sib)
    first = start_ref[0] - me * t
    both = 2 * t

    def ask(p):
        return pltpu.make_async_remote_copy(
            src_ref=piece(qseg, 0, p), dst_ref=piece(gq, 0, p),
            send_sem=gq_s.at[p], recv_sem=gq_r.at[p], device_id={"blk": z - 1},
        )

    def ask_low(p):
        return pltpu.make_async_remote_copy(
            src_ref=qseg.at[pl.ds(pl.multiple_of(p * t, t), sub), :],
            dst_ref=gq.at[pl.ds(pl.multiple_of(p * sub, sub), sub), :],
            send_sem=gq_s.at[p], recv_sem=gq_r.at[p], device_id={"blk": z - 1},
        )

    def cross(n):
        return pltpu.make_async_remote_copy(
            src_ref=piece(xsrc, 0, n), dst_ref=piece(xin, 0, n),
            send_sem=x_s.at[n], recv_sem=x_r.at[n], device_id={"blk": 2},
        )

    for jx, jc in arrival[1:]:
        source = partner(jx, jc)
        swap(0, kn, kbuf, 2 * seg, source, source).wait_recv()

        @pl.when(z != 0)
        def _():
            hop(piece(kbuf, 2 * seg, source), kbuf, 0, source).start()

    for jx, jc in arrival:
        source = partner(jx, jc)
        for part in range(2):
            swap_q(part, source, source).wait_recv()
    for copy in own_q:
        copy.wait()
    own_v.wait()
    own_k.wait()

    def choose(pair):
        later = first >= 2 * seg
        for part, buf in ((0, kbuf), (1, vbuf)):
            n = 2 * pair + part
            for h in range(heads):
                at = pl.ds(h * DH, DH)
                xsrc[pl.ds(n * t, t), at] = jnp.where(
                    later, qseg[pl.ds(n * t, t), at],
                    buf[pl.ds(2 * seg + (3 - pair) * t, t), at],
                )
            cross(n).start()

    @pl.when(z == 0)
    def _():
        choose(0)
        for jx, jc in arrival[1:]:
            source = partner(jx, jc)
            hop(piece(kbuf, 2 * seg, source), kbuf, 0, source).start()
        choose(1)

    for jx, jc in arrival[1:]:
        pass_back(1, partner(jx, jc))

    @pl.when(z == 3)
    def _():
        def send(step, carry):
            ask(nh - 1 - step).start()
            return carry

        lax.fori_loop(0, nh, send, 0)

    @pl.when(z == 2)
    def _():
        def send(step, carry):
            ask_low(nh - 1 - step).start()
            return carry

        lax.fori_loop(0, nh, send, 0)

    def weigh(q, keys, values, allowed):
        s = lax.dot_general(
            q, keys, (((1,), (1,)), ((), ())), preferred_element_type=jnp.float32
        )
        if allowed is not None:
            s = jnp.where(allowed, s, -1e30)
        peak = jnp.max(s, axis=1, keepdims=True)
        p = jnp.exp2(s - peak).astype(jnp.bfloat16)
        wide = jnp.concatenate([values, jnp.ones(values.shape, jnp.bfloat16)], axis=1)
        out = jnp.dot(p, wide, preferred_element_type=jnp.float32)
        return peak, out[:, DH:], out[:, :DH]

    def partial(size, q_of, k_of, v_of, allowed, put):
        lane = lax.broadcasted_iota(jnp.int32, (size, DH), 1)
        logs = jnp.zeros((size, DH), jnp.float32)
        for h in range(heads):
            at = pl.ds(h * DH, DH)
            peak, total, o = weigh(q_of(at), k_of(at), v_of(at), allowed)
            put(at, o / total)
            logs = jnp.where(lane == h, peak + jnp.log(total) * LOG2E, logs)
        return logs

    def cut(ref, base, size):
        rows = pl.ds(pl.multiple_of(base, sub), size)
        return lambda at: ref[rows, at]

    def into(ref, base, size):
        rows = pl.ds(pl.multiple_of(base, sub), size)

        def put(at, value):
            ref[rows, at] = value.astype(ref.dtype)

        return put

    def pair_rows(pair):
        return pl.ds(pl.multiple_of(pair * both, both), both)

    def ages(pair):
        r = lax.broadcasted_iota(jnp.int32, (both, seg), 0)
        upper = jnp.where(r < t + sub, r - sub, r + both - t)
        return jnp.where(r < sub, r, jnp.where(r < t, r + both - sub, upper)) + pair * t

    col = lax.broadcasted_iota(jnp.int32, (both, seg), 1)

    def own_part(pair, carry):
        own_log[pair_rows(pair), :] = partial(
            both, cut(qseg, pair * both, both), cut(kbuf, 2 * seg, seg), cut(vbuf, 2 * seg, seg),
            col <= ages(pair), into(acc, pair * both, both),
        )
        return carry

    lax.fori_loop(0, 2, own_part, 0)

    for jx, jc in arrival[1:]:
        pass_back(0, partner(jx, jc))
    loads[2].wait()

    def stats(e, p, to):
        return pltpu.make_async_remote_copy(
            src_ref=gst.at[e, p], dst_ref=gst_in.at[p],
            send_sem=st_s.at[e, p], recv_sem=st_r.at[p], device_id={"blk": to},
        )

    def answer(e, p, to):
        return [
            pltpu.make_async_remote_copy(
                src_ref=piece(go.at[e], 0, p), dst_ref=piece(gin, 0, p),
                send_sem=go_s.at[e, p], recv_sem=go_r.at[p], device_id={"blk": to},
            ),
            stats(e, p, to),
        ]

    def low_answer(p):
        return pltpu.make_async_remote_copy(
            src_ref=go.at[0, pl.ds(pl.multiple_of(p * sub, sub), sub), :],
            dst_ref=gin.at[pl.ds(pl.multiple_of(p * t, t), sub), :],
            send_sem=go_s.at[0, p], recv_sem=go_r.at[p], device_id={"blk": 2},
        )

    low_stats = pltpu.make_async_remote_copy(
        src_ref=low_log, dst_ref=low_in,
        send_sem=st_s.at[0, 0], recv_sem=st_r.at[0], device_id={"blk": 2},
    )

    def serve(e, pair, q_ref, base, to):
        logs = partial(
            both, cut(q_ref, pair * both, both), cut(kbuf, base, seg), cut(vbuf, base, seg),
            col > ages(pair), into(go.at[e], pair * both, both),
        ).T[:heads]
        for n in range(2):
            gst[e, 2 * pair + n] = logs[:, n * t:(n + 1) * t]
        for n in (1, 0):
            for copy in answer(e, 2 * pair + n, to):
                copy.start()

    def help_across(pair):
        for n in range(2):
            cross(2 * pair + n).wait_recv()
        serve(1, pair, xin, 2 * seg, 0)

    def help_next(pair):
        for n in range(2):
            ask(2 * pair + n).wait_recv()
        serve(0, pair, gq, seg, 3)

    @pl.when(z == 2)
    def _():
        help_across(0)

    def prev_in(i, carry):
        for kind in range(2):
            landed(bufs[kind], 0, kind, i).wait_recv()
        return carry

    lax.fori_loop(0, nh, prev_in, 0)

    turn[...] = jnp.zeros_like(turn)
    wide_turn[...] = jnp.zeros_like(wide_turn)

    @pl.when(z == 1)
    def _():
        for p in range(nh):
            ask_low(p).wait_recv()
        low_log[...] = partial(
            both, cut(gq, 0, both), cut(kbuf, seg, seg), cut(vbuf, seg, seg),
            col > lax.broadcasted_iota(jnp.int32, (both, seg), 0), into(go.at[0], 0, both),
        ).T[:heads]
        low_stats.start()
        for p in reversed(range(nh)):
            low_answer(p).start()

    def to_sibling(i, c):
        at = (i, slice(None), pl.ds(c * chunk, chunk))
        return pltpu.make_async_remote_copy(
            src_ref=sib_out.at[at], dst_ref=sib_in.at[at],
            send_sem=sib_s.at[i, c], recv_sem=sib_r.at[i, c],
            device_id={"head": sib},
        )

    def home(x, side, part, c):
        columns = pl.ds(pl.multiple_of(side * half + c * chunk, DH), chunk)
        return rbuf.at[x, pl.ds(pl.multiple_of(part * sub, sub), sub), columns]

    def strip(p, x, c):
        return comb.at[p, pl.ds(x * sub, sub), pl.ds(c * chunk, chunk)]

    def to_owner(p, x, c, source, owner):
        return pltpu.make_async_remote_copy(
            src_ref=strip(p, x, c), dst_ref=home(source // 2, source % 2, p % 2, c),
            send_sem=red_s.at[p, x, c], recv_sem=red_r.at[source, p % 2, c],
            device_id={"head": owner},
        )

    def keep(p, x, c):
        return pltpu.make_async_copy(
            strip(p, x, c), home(chip, core, p % 2, c), keep_sem.at[p % 2, c],
        )

    def near_part(pair, count):
        rows = [pl.ds((2 * pair + n) * t + sub, sub) for n in range(2)]

        def newest(first_slot):
            def of(at):
                last = xin[pl.ds(first_slot * t, t), at]
                if count == t:
                    return last
                return jnp.concatenate([xin[pl.ds((first_slot + 2) * t, t), at], last], axis=0)

            return of

        def put(at, value):
            for n in range(2):
                gin[rows[n], at] = value[n * sub:(n + 1) * sub].astype(gin.dtype)

        far_log[pl.ds(pair * t, t), :] = partial(
            t, lambda at: jnp.concatenate([qseg[rows[0], at], qseg[rows[1], at]], axis=0),
            newest(0), newest(1),
            lax.broadcasted_iota(jnp.int32, (t, count), 1)
            > lax.broadcasted_iota(jnp.int32, (t, count), 0), put,
        )

    def prev_part(pair):
        prev_log[pair_rows(pair), :] = partial(
            both, cut(qseg, pair * both, both), cut(kbuf, seg, seg), cut(vbuf, seg, seg), None,
            into(acc_prev, pair * both, both),
        )

    def turn_pair(step):
        pair = jnp.where(z == 0, step, 1 - step)

        @pl.when((z != 2) | (step == 0))
        def _():
            prev_part(pair)

        @pl.when(z == 1)
        def _():
            far_log[pair_rows(pair), :] = partial(
                both, cut(qseg, pair * both, both), cut(kbuf, 0, seg), cut(vbuf, 0, seg),
                col > ages(pair), into(gin, pair * both, both),
            )

        @pl.when((z == 2) & (step == 0))
        def _():
            help_next(1)
            near_part(1, t)
            help_next(0)
            prev_part(0)
            help_across(1)

        @pl.when((z == 2) & (step == 1))
        def _():
            near_part(0, both)

    def block(step, carry):
        @pl.when(step % 2 == 0)
        def _():
            turn_pair(step // 2)

        i = jnp.where(z == 0, step // 2 * 2 + 1 - step % 2, nh - 1 - step)
        rows = pl.ds(pl.multiple_of(i * t, t), t)

        @pl.when(z == 1)
        def _():
            near_log[...] = far_log[rows, :]

        @pl.when((z == 2) & (step == 0))
        def _():
            low_stats.wait_recv()
            wide_turn[:heads] = low_in[...]
            far_log[both:] = wide_turn[...].T

        @pl.when(z == 2)
        def _():
            low_answer(i).wait_recv()
            near_log[:sub] = far_log[pl.ds(pl.multiple_of(both + i * sub, sub), sub), :]
            near_log[sub:] = far_log[pl.ds(pl.multiple_of(i * sub, sub), sub), :]

        @pl.when((z == 0) | (z == 3))
        def _():
            for copy in answer(0, i, 0):
                copy.wait_recv()
            turn[:heads] = gst_in[i]
            near_log[...] = turn[...].T

        own = own_log[rows, :]
        before = jnp.where(first >= seg, prev_log[rows, :], -1e30)
        logs = jnp.where(first >= 2 * seg, near_log[...], -1e30)
        top = jnp.maximum(jnp.maximum(own, before), logs)
        own, before, logs = jnp.exp2(own - top), jnp.exp2(before - top), jnp.exp2(logs - top)
        share = 1.0 / (own + before + logs)
        own, before, logs = own * share, before * share, logs * share
        for h in range(heads):
            at = pl.ds(h * DH, DH)
            o = acc[rows, at] * own[:, h:h + 1] + acc_prev[rows, at] * before[:, h:h + 1]
            o = o + gin[rows, at].astype(jnp.float32) * logs[:, h:h + 1]
            ho[:, at] = o.astype(jnp.bfloat16)

        def project(side, c):
            at = pl.ds(pl.multiple_of(side * half + c * chunk, DH), chunk)
            return jnp.dot(ho[...], w_ref[:, at], preferred_element_type=jnp.float32)

        for c in range(NC):
            sib_out[i, :, pl.ds(c * chunk, chunk)] = project(1 - core, c).astype(jnp.bfloat16)
            to_sibling(i, c).start()
        for c in range(NC):
            at = pl.ds(c * chunk, chunk)
            mine = project(core, c)
            to_sibling(i, c).wait_recv()
            whole = mine + sib_in[i, :, at].astype(jnp.float32)
            comb[i, :, at] = whole.astype(jnp.bfloat16)
            for x in range(2):
                owner = i // 2 + 2 * x

                @pl.when(me == owner)
                def _():
                    keep(i, x, c).start()

                @pl.when(me != owner)
                def _():
                    to_owner(i, x, c, me, owner).start()

        return carry

    lax.fori_loop(0, nh, block, 0)

    for step in range(2):
        part = jnp.where(z == 0, step, 1 - step)
        for c in range(NC):
            keep((me % 2) * 2 + part, 0, c).wait()
            for jx, jc in arrival:
                source = partner(jx, jc)
                to_owner(part, 0, c, source, source).wait_recv()
            rows = pl.ds(pl.multiple_of(part * sub, sub), sub)
            for side in range(2):
                at = pl.ds(side * half + c * chunk, chunk)
                out_ref[rows, at] = (
                    rbuf[0, rows, at].astype(jnp.float32) + rbuf[1, rows, at].astype(jnp.float32)
                ).astype(out_ref.dtype)

    for jx, jc in arrival:
        peer = partner(jx, jc)
        swap(1, v_hbm, vbuf, 2 * seg, peer, me).wait_send()
        swap(0, kn, kbuf, 2 * seg, peer, me).wait_send()
        for part in range(2):
            swap_q(part, peer, me).wait_send()

    def sent(i, carry):
        for c in range(NC):
            to_sibling(i, c).wait_send()
            for x in range(2):
                owner = i // 2 + 2 * x

                @pl.when(me != owner)
                def _():
                    to_owner(i, x, c, me, owner).wait_send()

        @pl.when(z == 1)
        def _():
            for kind in range(2):
                relay(bufs[kind], kind, i).wait_send()

        return carry

    lax.fori_loop(0, nh, sent, 0)

    def hop_sent(i, carry):
        for kind in range(2):
            hop(piece(bufs[kind], 2 * seg, i), bufs[kind], kind, i).wait_send()
        return carry

    lax.fori_loop(0, nh, hop_sent, 0)

    @pl.when(z == 0)
    def _():
        for n in range(nh):
            cross(n).wait_send()

    @pl.when(z == 1)
    def _():
        low_stats.wait_send()
        for p in range(nh):
            low_answer(p).wait_send()

    @pl.when(z == 2)
    def _():
        for p in range(nh):
            ask_low(p).wait_send()
        for i in range(nh):
            for copy in answer(0, i, 3) + answer(1, i, 0):
                copy.wait_send()

    @pl.when(z == 3)
    def _():
        for i in range(nh):
            ask(i).wait_send()


def line_call(queries, keys, values, scale, w_out, stretch_start):
    nh = 4
    t, hd = queries.shape
    cols = hd // nh
    seg = nh * t
    width = w_out.shape[1]
    half = width // 2
    heads = cols // DH
    bf16 = jnp.bfloat16
    f32 = jnp.float32
    dma = pltpu.SemaphoreType.DMA
    anywhere = pl.BlockSpec(memory_space=pltpu.HBM)
    vmem = pl.BlockSpec(memory_space=pltpu.VMEM)
    return pl.pallas_call(
        line_kernel,
        out_shape=pltpu.VMEM((t, width), bf16),
        in_specs=[anywhere, anywhere, anywhere, vmem, anywhere,
                  pl.BlockSpec(memory_space=pltpu.SMEM)],
        out_specs=vmem,
        scratch_shapes=[
            pltpu.VMEM((nh // 2, t, width), bf16),
            pltpu.VMEM((t, hd), bf16),
            pltpu.VMEM((t, hd), bf16),
            pltpu.VMEM((t, hd), bf16),
            pltpu.VMEM((t, hd), bf16),
            pltpu.VMEM((cols, width), bf16),
            pltpu.VMEM((seg, cols), bf16),
            pltpu.VMEM((3 * seg, cols), bf16),
            pltpu.VMEM((3 * seg, cols), bf16),
            pltpu.VMEM((seg, cols), bf16),
            pltpu.VMEM((seg, cols), bf16),
            pltpu.VMEM((seg, cols), bf16),
            pltpu.VMEM((2, seg, cols), bf16),
            pltpu.VMEM((seg, cols), bf16),
            pltpu.VMEM((2, nh, heads, t), f32),
            pltpu.VMEM((nh, heads, t), f32),
            pltpu.VMEM((heads, 2 * t), f32),
            pltpu.VMEM((heads, 2 * t), f32),
            pltpu.VMEM((DH, t), f32),
            pltpu.VMEM((DH, 2 * t), f32),
            pltpu.VMEM((seg, DH), f32),
            pltpu.VMEM((t, DH), f32),
            pltpu.VMEM((seg, cols), f32),
            pltpu.VMEM((seg, DH), f32),
            pltpu.VMEM((seg, cols), f32),
            pltpu.VMEM((seg, DH), f32),
            pltpu.VMEM((t, cols), bf16),
            pltpu.VMEM((nh, t, half), bf16),
            pltpu.VMEM((nh, t, half), bf16),
            pltpu.VMEM((nh, t, half), bf16),
            dma((3,)),
            dma((4,)),
            dma((2, NC)),
            dma((2, nh)),
            dma((2, nh)),
            dma((2, nh)),
            dma((2, nh)),
            dma((2, nh)),
            dma((2, 2, nh)),
            dma((2, nh)),
            dma((nh,)),
            dma((nh,)),
            dma((nh,)),
            dma((nh,)),
            dma((2, nh)),
            dma((nh,)),
            dma((2, nh)),
            dma((nh,)),
            dma((nh, NC)),
            dma((nh, NC)),
            dma((nh, 2, NC)),
            dma((nh, 2, NC)),
        ],
        compiler_params=pltpu.CompilerParams(
            collective_id=0, has_side_effects=True,
            vmem_limit_bytes=54 * 1024 * 1024,
        ),
    )(queries, keys, values, scale, w_out, stretch_start)


def solution(mesh):
    nh = mesh.shape["head"]
    nb = mesh.shape["blk"]

    def shards(queries, keys, values, scale_qk, w_out, stretch_start):
        if nb == 4 and nh == 4:
            return line_call(
                queries, keys, values, scale_qk.reshape(1, -1), w_out, stretch_start
            )
        t, hd = queries.shape
        cols = hd // nh
        seg = nh * t
        width = w_out.shape[1]
        half = width // 2
        bf16 = jnp.bfloat16
        dma = pltpu.SemaphoreType.DMA
        anywhere = pl.BlockSpec(memory_space=pltpu.HBM)
        vmem = pl.BlockSpec(memory_space=pltpu.VMEM)
        parts = pl.pallas_call(
            functools.partial(kernel, nh, nb),
            out_shape=pltpu.VMEM((nh // 2, t, width), bf16),
            in_specs=[anywhere, anywhere, anywhere, vmem, anywhere,
                      pl.BlockSpec(memory_space=pltpu.SMEM)],
            out_specs=vmem,
            scratch_shapes=[
                pltpu.VMEM((t, hd), bf16),
                pltpu.VMEM((t, hd), bf16),
                pltpu.VMEM((t, hd), bf16),
                pltpu.VMEM((t, hd), bf16),
                pltpu.VMEM((cols, width), bf16),
                pltpu.VMEM((seg, cols), bf16),
                pltpu.VMEM((3 * seg, cols), bf16),
                pltpu.VMEM((3 * seg, cols), bf16),
                pltpu.VMEM((t, cols), jnp.float32),
                pltpu.VMEM((t, cols), bf16),
                pltpu.VMEM((nh, t, half), bf16),
                pltpu.VMEM((nh, t, half), bf16),
                pltpu.VMEM((nh, t, half), bf16),
                dma((3,)),
                dma((3,)),
                dma((NS, NC)),
                dma((3, nh)),
                dma((3, nh)),
                dma((2, nh)),
                dma((2, nh)),
                dma((2, nh, NS)),
                dma((2, nh, NS)),
                dma((nh, NS, NC)),
                dma((nh, NS, NC)),
                dma((nh, NS, NC)),
                dma((nh, NS, NC)),
            ],
            compiler_params=pltpu.CompilerParams(
                collective_id=0, has_side_effects=True, vmem_limit_bytes=54 * 1024 * 1024
            ),
        )(queries, keys, values, scale_qk.reshape(1, hd), w_out, stretch_start)
        return jnp.sum(parts.astype(jnp.float32), axis=0).astype(bf16)

    return jax.shard_map(
        shards,
        mesh=mesh,
        in_specs=(
            P(("groups", "blk", "head"), None),
            P(("groups", "blk", "head"), None),
            P(("groups", "blk", "head"), None),
            P(),
            P("head", None),
            P(("groups", "blk", "head")),
        ),
        out_specs=P(("groups", "blk", "head"), None),
        check_vma=False,
    )
```
